128 devices in a mesh: dp: 4 (over y), expert: 32 (over z, x, core).
Axes of the slice: x: 4, y: 4, z: 4, core: 2. Of those that a mesh axis runs over, the one named last changes fastest.
Arguments:
- tokens: bfloat16 [16384, 4096], P(('dp', 'expert')), may hold values from -6 to 6
- out_grad: bfloat16 [16384, 4096], P(('dp', 'expert')), may hold values from -6 to 6
- route_slots: int32 [4, 32, 32, 16], P('dp', 'expert'), may hold values from -1 to 127, as said below
- expert_counts: int32 [16384], P(('dp', 'expert')), may hold values from 0 to 32, as said below
- router_weight: float32 [4096, 32], replicated, may hold values from -0.09375 to 0.09375
- up_weight: bfloat16 [32, 4096, 1024], P('expert'), may hold values from -0.09375 to 0.09375
- down_weight: bfloat16 [32, 4096, 1024], P('expert'), may hold values from -0.1875 to 0.1875
Outputs:
- tokens_grad: bfloat16 [16384, 4096], P(('dp', 'expert'))
- up_grad: bfloat16 [32, 4096, 1024], P('expert', 'dp')
- down_grad: bfloat16 [32, 4096, 1024], P('expert', 'dp')
- router_grad: float32 [4096, 32], P(None, 'expert')
The draws below stay inside these ranges and needn't reach their ends.
Inputs may be any that keep to these rules, and one draw needn't show every extreme that they name: In route_slots[p, s, e, :] the chosen local tokens are distinct and come first, then -1; every list holds at least one token. In every batch shard some expert takes 16 tokens from every device of it. On every device one local token is chosen by every expert. expert_counts of a token equals the number of lists of route_slots that hold it.
All inputs are finite; a program needn't handle non-finite values.
Results may differ from the reference program's by a relative error of at most 0.017.
Values may be sent and summed in bfloat16 or wider, within the bound.
A program may use at most 192 MiB of HBM per device.

```python
import jax
import jax.numpy as jnp
from jax import lax

D = 4096
H = 1024
TOK_DEV = 128
EXPERTS = 32
RECV = 512
SLOT = 16
TOKENS = 16384
N_DP = 4
N_EXPERT = 32


def route_common(key):
    base = jax.random.fold_in(key, 7)
    key_count, key_full, key_perm, key_shared = jax.random.split(base, 4)
    counts = jax.random.randint(key_count, (N_DP, N_EXPERT, EXPERTS), 1, SLOT + 1)
    full = jax.random.randint(key_full, (N_DP,), 0, EXPERTS)
    chosen = jnp.arange(EXPERTS, dtype=jnp.int32)[None, None, :] == full[:, None, None]
    counts = jnp.where(chosen, SLOT, counts)
    shared = jax.random.randint(key_shared, (N_DP, N_EXPERT), 0, TOK_DEV).astype(jnp.int32)
    keys = jax.random.split(key_perm, N_DP * N_EXPERT * EXPERTS)
    perms = jax.vmap(lambda single: jax.random.permutation(single, TOK_DEV))(keys)
    perms = perms.reshape(N_DP, N_EXPERT, EXPERTS, TOK_DEV).astype(jnp.int32)
    hot = shared[:, :, None, None]
    first = perms[..., :1]
    perms = jnp.where(perms == hot, first, perms)
    places_all = jnp.arange(TOK_DEV, dtype=jnp.int32)[None, None, None, :]
    perms = jnp.where(places_all == 0, hot, perms)
    perms = perms[..., :SLOT]
    places = jnp.arange(SLOT, dtype=jnp.int32)[None, None, None, :]
    return jnp.where(places < counts[..., None], perms, -1).astype(jnp.int32)


def draw_route_slots(key, part):
    return route_common(key)


def draw_expert_counts(key, part):
    slots = route_common(key)
    hits = (slots[..., None] == jnp.arange(TOK_DEV, dtype=jnp.int32)).astype(jnp.int32)
    return jnp.sum(hits, axis=(2, 3)).reshape(TOKENS).astype(jnp.int32)


def steps_of(rng, dims, pieces, low, top_value):
    level, own = 1.0, jax.random.fold_in(rng, 6)
    for position, parts in pieces:
        heights = jnp.exp(jax.random.uniform(jax.random.fold_in(own, position), (parts,), jnp.float32, low / len(pieces), top_value / len(pieces)))
        level = level * jnp.repeat(heights, dims[position] // parts).reshape([-1 if axis == position else 1 for axis in range(len(dims))])
    return level


def gaussian(rng, dims, scale, most, cuts=(), held_as=jnp.bfloat16):
    values = jax.random.normal(rng, dims, jnp.float32) * scale
    if len(cuts) > 0:
        values = steps_of(rng, dims, cuts, -0.22, 0.18) * values
    return jnp.clip(values, min=-most, max=most).astype(held_as)


def setup_inputs(seed: int = 0) -> dict:
    key_of = jax.random.split(jax.random.key(seed), 8)
    return {
        "tokens": gaussian(key_of[0], (TOKENS, D), 1.0, 6.0, ((0, 128),)),
        "out_grad": gaussian(key_of[1], (TOKENS, D), 1.0, 6.0, ((0, 128),)),
        "route_slots": draw_route_slots(jax.random.fold_in(key_of[7], 71), 0),
        "expert_counts": draw_expert_counts(jax.random.fold_in(key_of[7], 71), 0),
        "router_weight": gaussian(key_of[4], (D, EXPERTS), D ** -0.5, 0.09375, (), jnp.float32),
        "up_weight": gaussian(key_of[5], (EXPERTS, D, H), D ** -0.5, 0.09375, ((0, 32),)),
        "down_weight": gaussian(key_of[6], (EXPERTS, D, H), H ** -0.5, 0.1875, ((0, 32),)),
    }


def gelu_pair(values):
    inner = 0.7978845608 * (values + 0.044715 * values * values * values)
    tangent = jnp.tanh(inner)
    result = 0.5 * values * (1.0 + tangent)
    slope = 0.5 * (1.0 + tangent) + 0.5 * values * (1.0 - tangent * tangent) * 0.7978845608 * (1.0 + 3.0 * 0.044715 * values * values)
    return result, slope


def reference(tokens, out_grad, route_slots, expert_counts, router_weight, up_weight, down_weight):
    group_rows = N_EXPERT * TOK_DEV
    width = tokens.shape[1]
    tok_groups = tokens.reshape(N_DP, group_rows, width)
    grad_groups = out_grad.reshape(N_DP, group_rows, width)
    count_groups = expert_counts.reshape(N_DP, group_rows).astype(jnp.float32)
    logits = jnp.dot(tokens.astype(jnp.float32), router_weight, precision=lax.Precision.HIGHEST)
    gates = jax.nn.sigmoid(logits).reshape(N_DP, group_rows, EXPERTS)
    source = (jnp.arange(N_EXPERT, dtype=jnp.int32) * TOK_DEV)[:, None]
    contract = (((0,), (0,)), ((), ()))
    trailing = (((1,), (1,)), ((), ()))

    def per_expert(carry, expert):
        row_acc, logit_acc = carry
        w_up = up_weight[expert]
        w_down = down_weight[expert]
        up_total = jnp.zeros((width, H), jnp.float32)
        down_total = jnp.zeros((width, H), jnp.float32)
        column = jnp.zeros((width,), jnp.float32)
        for group in range(N_DP):
            slots = route_slots[group, :, expert, :]
            valid = (slots >= 0).reshape(RECV)
            index = (source + jnp.maximum(slots, 0)).reshape(RECV).astype(jnp.int32)
            rows_in = jnp.where(valid[:, None], tok_groups[group][index], jnp.zeros((), tokens.dtype))
            grads_in = jnp.where(valid[:, None], grad_groups[group][index], jnp.zeros((), out_grad.dtype))
            gate_slot = jnp.where(valid, gates[group][index, expert], 0.0)
            count_slot = jnp.where(valid, count_groups[group][index], 1.0)
            weight_slot = jnp.where(valid, gate_slot / count_slot, 0.0)
            slope_slot = jnp.where(valid, gate_slot * (1.0 - gate_slot) / count_slot, 0.0)
            pre = jnp.dot(rows_in, w_up, preferred_element_type=jnp.float32)
            active, slope = gelu_pair(pre)
            active = active.astype(jnp.bfloat16)
            output = lax.dot_general(active, w_down, trailing, preferred_element_type=jnp.float32)
            score = jnp.sum(grads_in.astype(jnp.float32) * output, axis=1)
            out_scaled = (weight_slot[:, None] * grads_in.astype(jnp.float32)).astype(jnp.bfloat16)
            act_grad = jnp.dot(out_scaled, w_down, preferred_element_type=jnp.float32)
            pre_grad = (act_grad * slope).astype(jnp.bfloat16)
            row_grad = lax.dot_general(pre_grad, w_up, trailing, preferred_element_type=jnp.float32).astype(jnp.bfloat16)
            row_acc = row_acc.at[group, index].add(jnp.where(valid[:, None], row_grad.astype(jnp.float32), 0.0))
            logit_acc = logit_acc.at[group, index, expert].add(jnp.where(valid, score * slope_slot, 0.0))
            up_total = up_total + lax.dot_general(rows_in, pre_grad, contract, preferred_element_type=jnp.float32)
            down_total = down_total + lax.dot_general(out_scaled, active, contract, preferred_element_type=jnp.float32)
            column = column + jnp.dot(score * slope_slot, rows_in.astype(jnp.float32), precision=lax.Precision.HIGHEST)
        return (row_acc, logit_acc), (up_total.astype(jnp.bfloat16), down_total.astype(jnp.bfloat16), column)

    start = (jnp.zeros((N_DP, group_rows, width), jnp.float32), jnp.zeros((N_DP, group_rows, EXPERTS), jnp.float32))
    (row_acc, logit_acc), (up_grads, down_grads, columns) = lax.scan(per_expert, start, jnp.arange(EXPERTS, dtype=jnp.int32))
    logit_grad = logit_acc.reshape(TOKENS, EXPERTS)
    tokens_grad = (row_acc.reshape(TOKENS, width) + jnp.dot(logit_grad, router_weight.T, precision=lax.Precision.HIGHEST)).astype(jnp.bfloat16)
    return tokens_grad, up_grads, down_grads, columns.T
```

```python
import jax
import jax.numpy as jnp
from jax import lax
from jax.sharding import PartitionSpec as P

TRAIL = (((1,), (1,)), ((), ()))
ROWS = (((0,), (0,)), ((), ()))


def gelu_pair(values):
    inner = 0.7978845608 * (values + 0.044715 * values * values * values)
    tangent = jnp.tanh(inner)
    result = 0.5 * values * (1.0 + tangent)
    slope = 0.5 * (1.0 + tangent) + 0.5 * values * (1.0 - tangent * tangent) * 0.7978845608 * (
        1.0 + 3.0 * 0.044715 * values * values
    )
    return (result, slope)


def on_device(tokens, out_grad, route_slots, expert_counts, router_weight, up_weight, down_weight):
    experts = lax.axis_size("expert")
    n_dp = lax.axis_size("dp")
    me = lax.axis_index("expert")
    shard = lax.axis_index("dp")
    tok_rows, width = tokens.shape
    slots = route_slots[0, 0]
    per_slot = slots.shape[1]
    received = experts * per_slot
    highest = lax.Precision.HIGHEST
    piece = width // n_dp
    swap_a = [(0, 1), (1, 0), (2, 3), (3, 2)]
    swap_b = [(0, 3), (3, 0), (1, 2), (2, 1)]

    picks = slots[:, :, None] == jnp.arange(tok_rows, dtype=jnp.int32)[None, None, :]
    pick_half = picks.astype(jnp.bfloat16).reshape(received, tok_rows)

    def dispatch(rows):
        return lax.all_to_all(
            rows.reshape(experts, per_slot, width), "expert", split_axis=0, concat_axis=0, tiled=True
        ).reshape(received, width)

    with jax.named_scope("send_tokens"):
        rows_in = dispatch(
            jnp.dot(pick_half, tokens, preferred_element_type=jnp.float32).astype(jnp.bfloat16)
        )
    with jax.named_scope("send_grads"):
        logits = jnp.dot(tokens.astype(jnp.float32), router_weight, precision=highest)
        counts = jnp.maximum(expert_counts, 1).astype(jnp.float32)
        scaled = jax.nn.sigmoid(logits) / counts[:, None]
        weight_slot = jnp.sum(jnp.where(picks, scaled.T[:, None, :], 0.0), axis=2).reshape(received)
        picked = jnp.dot(pick_half, out_grad, preferred_element_type=jnp.float32)
        dout = dispatch((weight_slot[:, None] * picked).astype(jnp.bfloat16))

    def part(rows, index):
        return lax.dynamic_slice(rows, (0, index * piece), (received, piece))

    mate_a = shard ^ 1
    mate_b = n_dp - 1 - shard
    far = n_dp - 1 - mate_a
    w_up = up_weight[0]
    w_down = down_weight[0]
    with jax.named_scope("share_tokens"):
        rows_far = lax.ppermute(
            jnp.stack([part(rows_in, mate_a), part(rows_in, far)]), "dp", swap_a
        )
    with jax.named_scope("forward"):
        pre = jnp.dot(rows_in, w_up, preferred_element_type=jnp.float32)
        active, slope = gelu_pair(pre)
        active = active.astype(jnp.bfloat16)
        active_far = lax.ppermute(active, "dp", swap_b)
        column = lax.dynamic_slice(router_weight, (0, me), (width, 1))[:, 0]
        rows_float = rows_in.astype(jnp.float32)
        gate = jax.nn.sigmoid(jnp.sum(rows_float * column[None, :], axis=1))
    with jax.named_scope("share_grads"):
        dout_far = lax.ppermute(jnp.stack([part(dout, mate_b), part(dout, far)]), "dp", swap_b)
    with jax.named_scope("backward"):
        act_grad = jnp.dot(dout, w_down, preferred_element_type=jnp.float32)
        logit_grad = (1.0 - gate) * jnp.sum(active.astype(jnp.float32) * act_grad, axis=1)
        pre_grad = (act_grad * slope).astype(jnp.bfloat16)
        pre_grad_far = lax.ppermute(pre_grad, "dp", swap_a)
        row_grad = lax.dot_general(pre_grad, w_up, TRAIL, preferred_element_type=jnp.float32)
        row_grad = (row_grad + logit_grad[:, None] * column[None, :]).astype(jnp.bfloat16)
    with jax.named_scope("return_rows"):
        back_rows = dispatch(row_grad)
    with jax.named_scope("weight_grads"):

        def product(left, right, left_far, right_far):
            return lax.dot_general(
                left, right, ROWS, preferred_element_type=jnp.float32
            ) + lax.dot_general(left_far, right_far, ROWS, preferred_element_type=jnp.float32)

        down_send = product(part(dout, mate_a), active, dout_far[1], active_far)
        down_got = lax.ppermute(down_send.astype(jnp.bfloat16), "dp", swap_a)
        up_send = product(part(rows_in, mate_b), pre_grad, rows_far[1], pre_grad_far)
        up_got = lax.ppermute(up_send.astype(jnp.bfloat16), "dp", swap_b)
        down_own = product(part(dout, shard), active, dout_far[0], active_far)
        up_own = product(part(rows_in, shard), pre_grad, rows_far[0], pre_grad_far)
        down_sum = (down_own + down_got.astype(jnp.float32)).astype(jnp.bfloat16)
        up_sum = (up_own + up_got.astype(jnp.float32)).astype(jnp.bfloat16)
    with jax.named_scope("router_grad"):
        terms = jnp.sum(rows_float * logit_grad[:, None], axis=0)
        terms = terms + lax.ppermute(terms, "dp", swap_a)
        terms = terms + lax.ppermute(terms, "dp", swap_b)
    with jax.named_scope("tokens_grad"):
        tokens_grad = lax.dot_general(
            pick_half, back_rows, ROWS, preferred_element_type=jnp.float32
        ).astype(jnp.bfloat16)
    return (tokens_grad, up_sum[None], down_sum[None], terms[:, None])


def solution(mesh):
    return jax.shard_map(
        on_device,
        mesh=mesh,
        in_specs=(
            P(("dp", "expert"), None),
            P(("dp", "expert"), None),
            P("dp", "expert", None, None),
            P(("dp", "expert")),
            P(),
            P("expert", None, None),
            P("expert", None, None),
        ),
        out_specs=(
            P(("dp", "expert"), None),
            P("expert", "dp", None),
            P("expert", "dp", None),
            P(None, "expert"),
        ),
        check_vma=False,
    )
```

```python
import functools

import jax
import jax.numpy as jnp
from jax import lax
from jax.experimental import pallas as pl
from jax.experimental.pallas import tpu as pltpu
from jax.sharding import PartitionSpec as P

MESH = pl.DeviceIdType.MESH
TRAIL = (((1,), (1,)), ((), ()))
ROWS = (((0,), (0,)), ((), ()))
WAVES = (
    ((1, 1), (3, 3), (1, 3), (3, 1)),
    ((0, 0), (2, 2), (2, 0), (0, 2)),
    ((1, 0), (3, 0), (1, 2), (3, 2)),
    ((0, 1), (0, 3), (2, 1), (2, 3)),
)
STEPS = tuple((dz, dx, dc) for wave in WAVES for dz, dx in wave for dc in (0, 1))
SELF = STEPS.index((0, 0, 0))
PER_WAVE = 8
PIECES = 4


def shifted(me, step, sign):
    dz, dx, dc = step
    z, x, c = me // 8, (me // 2) % 4, me % 2
    z = (z + sign * dz + 4) % 4
    x = (x + sign * dx + 4) % 4
    c = (c + sign * dc + 2) % 2
    return (z * 4 + x) * 2 + c


def gelu_pair(values):
    inner = 0.7978845608 * (values + 0.044715 * values * values * values)
    tangent = jnp.tanh(inner)
    result = 0.5 * values * (1.0 + tangent)
    slope = 0.5 * (1.0 + tangent) + 0.5 * values * (1.0 - tangent * tangent) * 0.7978845608 * (
        1.0 + 3.0 * 0.044715 * values * values
    )
    return (result, slope)


def kernel(
    tokens, grads, pick, pick_back, weight, column, up_hbm, down_hbm,
    tokens_grad, up_out, down_out, terms_out,
    x_send, g_send, x_in, g_in, r_in, w_up, w_down, act, slope, dpre, logit,
    x_far, dpre_far, g_far, act_far, up_send, down_send, up_got, down_got, up_own, down_own,
    terms_a, terms_b,
    w_sem, xs_sem, xr_sem, gs_sem, gr_sem, rs_sem, rr_sem,
    xfs_sem, xfr_sem, dfs_sem, dfr_sem, gfs_sem, gfr_sem, afs_sem, afr_sem,
    ups_sem, upr_sem, dns_sem, dnr_sem, ts_sem, tr_sem, out_sem,
):
    shard = lax.axis_index("dp")
    me = lax.axis_index("expert")
    mate_a = shard + 1 - 2 * (shard % 2)
    mate_b = 3 - shard
    far = 3 - mate_a
    width = tokens.shape[1]
    hidden = act.shape[1]
    piece = width // 4
    block = 16
    wave_rows = PER_WAVE * block
    step_rows = piece // PIECES

    load_up = pltpu.make_async_copy(up_hbm, w_up, w_sem.at[0])
    load_down = pltpu.make_async_copy(down_hbm, w_down, w_sem.at[1])
    load_up.start()
    load_down.start()

    barrier = pltpu.get_barrier_semaphore()
    for step in STEPS:
        if step != (0, 0, 0):
            pl.semaphore_signal(
                barrier, inc=1, device_id=(shard, shifted(me, step, 1)), device_id_type=MESH
            )
    pl.semaphore_signal(barrier, inc=1, device_id=(mate_a, me), device_id_type=MESH)
    pl.semaphore_signal(barrier, inc=1, device_id=(mate_b, me), device_id_type=MESH)
    pl.semaphore_wait(barrier, len(STEPS) + 1)

    def span(w):
        return pl.ds(w * wave_rows, wave_rows)

    def columns(index, size=piece, offset=0):
        return pl.ds(pl.multiple_of(index * piece + offset, 128), size)

    def arrived(ref, sem):
        pltpu.make_async_copy(ref, ref, sem).wait()

    def remote(src, dst, send, recv, device):
        copy = pltpu.make_async_remote_copy(
            src_ref=src, dst_ref=dst, send_sem=send, recv_sem=recv,
            device_id=device, device_id_type=MESH,
        )
        copy.start()

    def wave_part(w):
        if SELF // PER_WAVE == w:
            return pl.ds(w * wave_rows + block, wave_rows - block)
        return span(w)

    def send_blocks(w, sign, src, dst, send, recv):
        for k in range(w * PER_WAVE, (w + 1) * PER_WAVE):
            if k != SELF:
                rows = pl.ds(k * block, block)
                remote(
                    src.at[rows], dst.at[rows], send.at[w], recv.at[w],
                    (shard, shifted(me, STEPS[k], sign)),
                )

    def own_block(w, src, dst):
        if SELF // PER_WAVE == w:
            rows = pl.ds(SELF * block, block)
            dst[rows, :] = src[rows, :]

    for w in range(4):
        @pl.loop(0, 4)
        def _(n):
            cols = columns(n)
            picked = jnp.dot(
                pick[span(w), :], tokens[:, cols], preferred_element_type=jnp.float32
            )
            x_send[span(w), cols] = picked.astype(jnp.bfloat16)

        send_blocks(w, 1, x_send, x_in, xs_sem, xr_sem)
        own_block(w, x_send, x_in)

        @pl.loop(0, 4)
        def _(n):
            cols = columns(n)
            picked = jnp.dot(
                pick[span(w), :], grads[:, cols], preferred_element_type=jnp.float32
            )
            g_send[span(w), cols] = (weight[span(w), :] * picked).astype(jnp.bfloat16)

        send_blocks(w, 1, g_send, g_in, gs_sem, gr_sem)
        own_block(w, g_send, g_in)

    load_up.wait()
    load_down.wait()
    for w in range(4):
        rows = span(w)
        arrived(x_in.at[wave_part(w)], xr_sem.at[w])
        for slot, index in ((1, far), (0, mate_a)):
            remote(
                x_in.at[rows, columns(index)], x_far.at[slot, rows],
                xfs_sem.at[w], xfr_sem.at[w], (mate_a, me),
            )

        @pl.loop(0, 4)
        def _(n):
            cols = pl.ds(pl.multiple_of(n * 256, 256), 256)
            pre = jnp.dot(x_in[rows, :], w_up[:, cols], preferred_element_type=jnp.float32)
            active, bend = gelu_pair(pre)
            act[rows, cols] = active.astype(jnp.bfloat16)
            slope[:, cols] = bend

        remote(act.at[rows], act_far.at[rows], afs_sem.at[w], afr_sem.at[w], (mate_b, me))
        gate = jnp.zeros((wave_rows, 1), jnp.float32)
        for n in range(4):
            cols = pl.ds(n * piece, piece)
            gate = gate + jnp.sum(
                x_in[rows, cols].astype(jnp.float32) * column[:, cols], axis=1, keepdims=True
            )
        closed = 1.0 - jax.nn.sigmoid(gate)
        arrived(g_in.at[wave_part(w)], gr_sem.at[w])
        for slot, index in ((1, far), (0, mate_b)):
            remote(
                g_in.at[rows, columns(index)], g_far.at[slot, rows],
                gfs_sem.at[w], gfr_sem.at[w], (mate_b, me),
            )
        logit[rows, :] = jnp.zeros((wave_rows, 1), jnp.float32)

        @pl.loop(0, 4)
        def _(n):
            cols = pl.ds(pl.multiple_of(n * 256, 256), 256)
            back = jnp.dot(g_in[rows, :], w_down[:, cols], preferred_element_type=jnp.float32)
            logit[rows, :] += jnp.sum(
                act[rows, cols].astype(jnp.float32) * back, axis=1, keepdims=True
            )
            dpre[rows, cols] = (back * slope[:, cols]).astype(jnp.bfloat16)

        remote(dpre.at[rows], dpre_far.at[rows], dfs_sem.at[w], dfr_sem.at[w], (mate_a, me))
        logit[rows, :] = logit[rows, :] * closed
        arrived(x_send.at[wave_part(w)], xs_sem.at[w])

        @pl.loop(0, 8)
        def _(n):
            cols = pl.ds(pl.multiple_of(n * 512, 512), 512)
            partial = lax.dot_general(
                dpre[rows, :], w_up[cols, :], TRAIL, preferred_element_type=jnp.float32
            )
            partial = partial + logit[rows, :] * column[:, cols]
            x_send[rows, cols] = partial.astype(jnp.bfloat16)

        send_blocks(w, -1, x_send, r_in, rs_sem, rr_sem)
        own_block(w, x_send, r_in)

    def product(left, index, right, left_far, slot, right_far, i, n):
        cols = pl.ds(pl.multiple_of(n * 512, 512), 512)
        offset = i * step_rows
        near = lax.dot_general(
            left[:, columns(index, step_rows, offset)], right[:, cols], ROWS,
            preferred_element_type=jnp.float32,
        )
        other = lax.dot_general(
            left_far[slot, :, pl.ds(offset, step_rows)], right_far[:, cols], ROWS,
            preferred_element_type=jnp.float32,
        )
        return cols, near + other

    for w in range(4):
        arrived(g_far.at[:, span(w)], gfr_sem.at[w])
        arrived(act_far.at[span(w)], afr_sem.at[w])
        arrived(x_far.at[:, span(w)], xfr_sem.at[w])
        arrived(dpre_far.at[span(w)], dfr_sem.at[w])
    for i in range(PIECES):
        part = pl.ds(i * step_rows, step_rows)

        @pl.loop(0, 2)
        def _(n):
            cols, value = product(g_in, mate_a, act, g_far, 1, act_far, i, n)
            down_send[part, cols] = value.astype(jnp.bfloat16)

        remote(down_send.at[part], down_got.at[part], dns_sem.at[i], dnr_sem.at[i], (mate_a, me))

        @pl.loop(0, 2)
        def _(n):
            cols, value = product(x_in, mate_b, dpre, x_far, 1, dpre_far, i, n)
            up_send[part, cols] = value.astype(jnp.bfloat16)

        remote(up_send.at[part], up_got.at[part], ups_sem.at[i], upr_sem.at[i], (mate_b, me))

    for n in range(8):
        cols = pl.ds(n * 512, 512)
        terms_a[0:1, cols] = jnp.sum(
            x_in[:, cols].astype(jnp.float32) * logit[...], axis=0, keepdims=True
        )
    remote(terms_a.at[0:1], terms_a.at[1:2], ts_sem.at[0], tr_sem.at[0], (mate_a, me))
    arrived(terms_a.at[1:2], tr_sem.at[0])
    terms_b[0:1, :] = terms_a[0:1, :] + terms_a[1:2, :]
    remote(terms_b.at[0:1], terms_b.at[1:2], ts_sem.at[1], tr_sem.at[1], (mate_b, me))
    arrived(terms_b.at[1:2], tr_sem.at[1])
    terms_out[...] = terms_b[0:1, :] + terms_b[1:2, :]

    for i in range(PIECES):
        part = pl.ds(i * step_rows, step_rows)
        if i == PIECES - 1:
            for w in range(4):
                arrived(r_in.at[wave_part(w)], rr_sem.at[w])

            @pl.loop(0, 8)
            def _(n):
                cols = pl.ds(pl.multiple_of(n * 512, 512), 512)
                tokens_grad[:, cols] = jnp.dot(
                    pick_back[...], r_in[:, cols], preferred_element_type=jnp.float32
                ).astype(jnp.bfloat16)

        arrived(down_got.at[part], dnr_sem.at[i])

        @pl.loop(0, 2)
        def _(n):
            cols, value = product(g_in, shard, act, g_far, 0, act_far, i, n)
            value = value + down_got[part, cols].astype(jnp.float32)
            down_own[part, cols] = value.astype(jnp.bfloat16)

        pltpu.make_async_copy(down_own.at[part], down_out.at[part], out_sem.at[0, i]).start()
        arrived(up_got.at[part], upr_sem.at[i])

        @pl.loop(0, 2)
        def _(n):
            cols, value = product(x_in, shard, dpre, x_far, 0, dpre_far, i, n)
            value = value + up_got[part, cols].astype(jnp.float32)
            up_own[part, cols] = value.astype(jnp.bfloat16)

        pltpu.make_async_copy(up_own.at[part], up_out.at[part], out_sem.at[1, i]).start()

    for w in range(4):
        arrived(g_send.at[wave_part(w)], gs_sem.at[w])
        arrived(x_send.at[wave_part(w)], rs_sem.at[w])
        arrived(x_far.at[:, span(w)], xfs_sem.at[w])
        arrived(g_far.at[:, span(w)], gfs_sem.at[w])
        arrived(act.at[span(w)], afs_sem.at[w])
        arrived(dpre.at[span(w)], dfs_sem.at[w])
    arrived(terms_a.at[0:1], ts_sem.at[0])
    arrived(terms_b.at[0:1], ts_sem.at[1])
    for i in range(PIECES):
        part = pl.ds(i * step_rows, step_rows)
        arrived(down_send.at[part], dns_sem.at[i])
        arrived(up_send.at[part], ups_sem.at[i])
        pltpu.make_async_copy(down_own.at[part], down_out.at[part], out_sem.at[0, i]).wait()
        pltpu.make_async_copy(up_own.at[part], up_out.at[part], out_sem.at[1, i]).wait()


def on_device(tokens, out_grad, route_slots, expert_counts, router_weight, up_weight, down_weight):
    me = lax.axis_index("expert")
    tok_rows, width = tokens.shape
    hidden = up_weight.shape[2]
    piece = width // 4
    slots = route_slots[0, 0]
    experts, per_slot = slots.shape
    received = experts * per_slot
    with jax.named_scope("gates"):
        order = jnp.stack([shifted(me, step, 1) for step in STEPS])
        slots = slots[order]
        picks = slots[:, :, None] == jnp.arange(tok_rows, dtype=jnp.int32)[None, None, :]
        pick = picks.astype(jnp.bfloat16).reshape(received, tok_rows)
        pick_back = pick.T
        logits = jnp.dot(
            tokens.astype(jnp.float32), router_weight, precision=lax.Precision.HIGHEST
        )
        counts = jnp.maximum(expert_counts, 1).astype(jnp.float32)
        scaled = (jax.nn.sigmoid(logits) / counts[:, None]).T[order]
        weight = jnp.sum(jnp.where(picks, scaled[:, None, :], 0.0), axis=2).reshape(received, 1)
        column = lax.dynamic_slice(router_weight, (0, me), (width, 1)).reshape(1, width)

    half = jnp.bfloat16
    vmem = pl.BlockSpec(memory_space=pltpu.VMEM)
    anywhere = pl.BlockSpec(memory_space=pl.ANY)
    dma = pltpu.SemaphoreType.DMA
    rows_buffer = pltpu.VMEM((received, width), half)
    inner = pltpu.VMEM((received, hidden), half)
    halves = pltpu.VMEM((2, received, piece), half)
    square = pltpu.VMEM((piece, hidden), half)
    full = pltpu.VMEM((width, hidden), half)
    tokens_grad, up_sum, down_sum, terms = pl.pallas_call(
        kernel,
        out_shape=(
            jax.ShapeDtypeStruct((tok_rows, width), half),
            jax.ShapeDtypeStruct((piece, hidden), half),
            jax.ShapeDtypeStruct((piece, hidden), half),
            jax.ShapeDtypeStruct((1, width), jnp.float32),
        ),
        in_specs=[vmem] * 6 + [anywhere] * 2,
        out_specs=(vmem, anywhere, anywhere, vmem),
        scratch_shapes=[
            rows_buffer, rows_buffer, rows_buffer, rows_buffer, rows_buffer, full, full,
            inner, pltpu.VMEM((PER_WAVE * per_slot, hidden), jnp.float32), inner,
            pltpu.VMEM((received, 1), jnp.float32),
            halves, inner, halves, inner, square, square, square, square, square, square,
            pltpu.VMEM((2, width), jnp.float32), pltpu.VMEM((2, width), jnp.float32),
            dma((2,)),
        ]
        + [dma((4,))] * 14
        + [dma((PIECES,))] * 4
        + [dma((2,)), dma((2,)), dma((2, PIECES))],
        compiler_params=pltpu.CompilerParams(
            collective_id=0, has_side_effects=True, vmem_limit_bytes=67043328
        ),
        name="exchange",
    )(tokens, out_grad, pick, pick_back, weight, column, up_weight[0], down_weight[0])
    return (tokens_grad, up_sum[None], down_sum[None], terms.reshape(width, 1))


def solution(mesh):
    return jax.shard_map(
        on_device,
        mesh=mesh,
        in_specs=(
            P(("dp", "expert"), None),
            P(("dp", "expert"), None),
            P("dp", "expert", None, None),
            P(("dp", "expert")),
            P(),
            P("expert", None, None),
            P("expert", None, None),
        ),
        out_specs=(
            P(("dp", "expert"), None),
            P("expert", "dp", None),
            P("expert", "dp", None),
            P(None, "expert"),
        ),
        check_vma=False,
    )
```

```python
import functools

import jax
import jax.numpy as jnp
from jax import lax
from jax.experimental import pallas as pl
from jax.experimental.pallas import tpu as pltpu
from jax.sharding import PartitionSpec as P

MESH = pl.DeviceIdType.MESH
TRAIL = (((1,), (1,)), ((), ()))
ROWS = (((0,), (0,)), ((), ()))
WAVES = (
    ((1, 1), (3, 3), (1, 3), (3, 1)),
    ((2, 1), (2, 3), (1, 0), (3, 0)),
    ((1, 2), (3, 2), (0, 1), (0, 3)),
    ((0, 0), (2, 2), (2, 0), (0, 2)),
)
STEPS = tuple((dz, dx, dc) for wave in WAVES for dz, dx in wave for dc in (0, 1))
COUNTS = tuple(2 * len(wave) for wave in WAVES)
FIRST = tuple(sum(COUNTS[:w]) for w in range(len(WAVES)))
SELF = STEPS.index((0, 0, 0))
N_WAVES = len(WAVES)
BLOCK = 16
CHUNKS = tuple(
    tuple(range(first, first + count, count if w < N_WAVES - 1 else 2))
    for w, (first, count) in enumerate(zip(FIRST, COUNTS))
)
CHUNK_OF = tuple(
    sum(1 for chunks in CHUNKS for start in chunks if start <= k) - 1 for k in range(len(STEPS))
)
WAVE_OF = tuple(sum(1 for first in FIRST if first <= k) - 1 for k in range(len(STEPS)))
N_CHUNKS = CHUNK_OF[-1] + 1
PIECES = 4


def shifted(me, step, sign):
    dz, dx, dc = step
    z, x, c = me // 8, (me // 2) % 4, me % 2
    other = (c + dc) % 2
    swap = c if sign > 0 else other
    z = (z + sign * (dz + swap * (dx - dz)) + 4) % 4
    x = (x + sign * (dx + swap * (dz - dx)) + 4) % 4
    return (z * 4 + x) * 2 + other


def gelu_pair(values):
    inner = 0.7978845608 * (values + 0.044715 * values * values * values)
    tangent = jnp.tanh(inner)
    result = 0.5 * values * (1.0 + tangent)
    slope = 0.5 * (1.0 + tangent) + 0.5 * values * (1.0 - tangent * tangent) * 0.7978845608 * (
        1.0 + 3.0 * 0.044715 * values * values
    )
    return (result, slope)


def kernel(
    tokens, grads, slots, counts, router, up_hbm, down_hbm,
    tokens_grad, up_out, down_out, terms_out,
    pick, pick_back, scaled, column,
    x_send, g_send, x_in, g_in, r_in, w_up, w_down, act, slope, dpre, logit,
    x_far, dpre_far, g_far, act_far, up_send, down_send, up_got, down_got, own_sum,
    terms_a, terms_b,
    w_sem, xs_sem, xr_sem, gs_sem, gr_sem, rs_sem, rr_sem,
    xfs_sem, xfr_sem, dfs_sem, dfr_sem, gfs_sem, gfr_sem, afs_sem, afr_sem,
    ups_sem, upr_sem, dns_sem, dnr_sem, ts_sem, tr_sem, out_sem,
):
    shard = lax.axis_index("dp")
    me = lax.axis_index("expert")
    mate_a = shard + 1 - 2 * (shard % 2)
    mate_b = 3 - shard
    far = 3 - mate_a
    width = tokens.shape[1]
    hidden = act.shape[1]
    piece = width // 4
    step_rows = piece // PIECES

    load_up = pltpu.make_async_copy(up_hbm, w_up, w_sem.at[0])
    load_down = pltpu.make_async_copy(down_hbm, w_down, w_sem.at[1])
    load_up.start()
    load_down.start()

    barrier = pltpu.get_barrier_semaphore()
    for step in STEPS:
        if step != (0, 0, 0):
            pl.semaphore_signal(
                barrier, inc=1, device_id=(shard, shifted(me, step, 1)), device_id_type=MESH
            )
    pl.semaphore_signal(barrier, inc=1, device_id=(mate_a, me), device_id_type=MESH)
    pl.semaphore_signal(barrier, inc=1, device_id=(mate_b, me), device_id_type=MESH)

    def span(w):
        return pl.ds(FIRST[w] * BLOCK, COUNTS[w] * BLOCK)

    def columns(index, size=piece, offset=0):
        return pl.ds(pl.multiple_of(index * piece + offset, 128), size)

    def arrived(ref, sem):
        pltpu.make_async_copy(ref, ref, sem).wait()

    def remote(src, dst, send, recv, device):
        copy = pltpu.make_async_remote_copy(
            src_ref=src, dst_ref=dst, send_sem=send, recv_sem=recv,
            device_id=device, device_id_type=MESH,
        )
        copy.start()

    def travels(w):
        if FIRST[w] == SELF:
            return pl.ds((SELF + 1) * BLOCK, (COUNTS[w] - 1) * BLOCK)
        return span(w)

    def chunk_rows(start, traveled):
        count = sum(1 for k in CHUNK_OF if k == CHUNK_OF[start])
        skip = 1 if traveled and start == SELF else 0
        return pl.ds((start + skip) * BLOCK, (count - skip) * BLOCK)

    def send_blocks(w, src, dst, send, recv, tags):
        for k in range(FIRST[w], FIRST[w] + COUNTS[w]):
            rows = pl.ds(k * BLOCK, BLOCK)
            if k == SELF:
                dst[rows, :] = src[rows, :]
            else:
                remote(
                    src.at[rows], dst.at[rows], send.at[w], recv.at[tags[k]],
                    (shard, shifted(me, STEPS[k], 1)),
                )

    def return_blocks(w, src, dst, send, recv):
        for k in range(FIRST[w], FIRST[w] + COUNTS[w]):
            rows = pl.ds(k * BLOCK, BLOCK)
            home = pl.ds(pl.multiple_of(me * BLOCK, BLOCK), BLOCK)
            if k == SELF:
                dst[home, :] = src[rows, :]
            else:
                remote(
                    src.at[rows], dst.at[home], send.at[w], recv.at[w],
                    (shard, shifted(me, STEPS[k], -1)),
                )

    def add_terms(w):
        rows = span(w)
        for n in range(8):
            cols = pl.ds(n * 512, 512)
            value = jnp.sum(
                x_in[rows, cols].astype(jnp.float32) * logit[rows, :], axis=0, keepdims=True
            )
            terms_a[0:1, cols] = value if w == 0 else terms_a[0:1, cols] + value

    def wave_steps(w):
        return [shifted(me, STEPS[k], 1) for k in range(FIRST[w], FIRST[w] + COUNTS[w])]

    def wave_picks(w):
        return [pick[pl.ds(pl.multiple_of(to * BLOCK, BLOCK), BLOCK), :] for to in wave_steps(w)]

    def select_tokens(w):
        chosen = jnp.concatenate(wave_picks(w), axis=0)

        @pl.loop(0, 4)
        def _(n):
            cols = columns(n)
            picked = jnp.dot(chosen, tokens[:, cols], preferred_element_type=jnp.float32)
            x_send[span(w), cols] = picked.astype(jnp.bfloat16)

    def select_grads(w):
        picks = wave_picks(w)
        chosen = jnp.concatenate(picks, axis=0)
        weight = jnp.concatenate(
            [
                jnp.sum(one.astype(jnp.float32) * scaled[pl.ds(to, 1), :], axis=1, keepdims=True)
                for one, to in zip(picks, wave_steps(w))
            ],
            axis=0,
        )

        @pl.loop(0, 4)
        def _(n):
            cols = columns(n)
            picked = jnp.dot(chosen, grads[:, cols], preferred_element_type=jnp.float32)
            g_send[span(w), cols] = (weight * picked).astype(jnp.bfloat16)

    tok_rows = tokens.shape[0]
    places = lax.broadcasted_iota(jnp.int32, (tok_rows, slots.shape[1]), 0)
    hits = jnp.where(places == slots[...], 1.0, 0.0)
    pick_back[...] = hits.astype(jnp.bfloat16)
    pick[...] = hits.T.astype(jnp.bfloat16)
    select_tokens(0)
    pl.semaphore_wait(barrier, len(STEPS) + 1)
    send_blocks(0, x_send, x_in, xs_sem, xr_sem, WAVE_OF)

    logits = jnp.zeros((router.shape[0], tok_rows), jnp.float32)
    rest = router[...]
    for _ in range(3):
        head = rest.astype(jnp.bfloat16)
        rest = rest - head.astype(jnp.float32)
        logits = logits + lax.dot_general(
            head, tokens[...], TRAIL, preferred_element_type=jnp.float32
        )
    tallies = jnp.maximum(counts[...], 1).astype(jnp.float32)
    scaled[...] = jax.nn.sigmoid(logits) / tallies
    column[...] = router[pl.ds(me, 1), :]
    for w in range(N_WAVES):
        if w > 0:
            select_tokens(w)
            send_blocks(w, x_send, x_in, xs_sem, xr_sem, WAVE_OF)
        select_grads(w)
        send_blocks(w, g_send, g_in, gs_sem, gr_sem, CHUNK_OF)

    load_up.wait()
    load_down.wait()
    for w in range(N_WAVES):
        rows = span(w)
        wave_rows = COUNTS[w] * BLOCK
        arrived(x_in.at[travels(w)], xr_sem.at[w])
        for slot, index in ((1, far), (0, mate_a)):
            remote(
                x_in.at[rows, columns(index)], x_far.at[slot, rows],
                xfs_sem.at[w], xfr_sem.at[w], (mate_a, me),
            )

        @pl.loop(0, 4)
        def _(n):
            cols = pl.ds(pl.multiple_of(n * 256, 256), 256)
            pre = jnp.dot(x_in[rows, :], w_up[:, cols], preferred_element_type=jnp.float32)
            active, bend = gelu_pair(pre)
            act[rows, cols] = active.astype(jnp.bfloat16)
            slope[0:wave_rows, cols] = bend

        remote(act.at[rows], act_far.at[rows], afs_sem.at[w], afr_sem.at[w], (mate_b, me))
        gate = jnp.zeros((wave_rows, 1), jnp.float32)
        for n in range(4):
            cols = pl.ds(n * piece, piece)
            gate = gate + jnp.sum(
                x_in[rows, cols].astype(jnp.float32) * column[:, cols], axis=1, keepdims=True
            )
        closed = 1.0 - jax.nn.sigmoid(gate)
        for start in CHUNKS[w]:
            tag = CHUNK_OF[start]
            arrived(g_in.at[chunk_rows(start, True)], gr_sem.at[tag])
            some = chunk_rows(start, False)
            for slot, index in ((1, far), (0, mate_b)):
                remote(
                    g_in.at[some, columns(index)], g_far.at[slot, some],
                    gfs_sem.at[tag], gfr_sem.at[tag], (mate_b, me),
                )
        logit[rows, :] = jnp.zeros((wave_rows, 1), jnp.float32)

        @pl.loop(0, 4)
        def _(n):
            cols = pl.ds(pl.multiple_of(n * 256, 256), 256)
            back = jnp.dot(g_in[rows, :], w_down[:, cols], preferred_element_type=jnp.float32)
            logit[rows, :] += jnp.sum(
                act[rows, cols].astype(jnp.float32) * back, axis=1, keepdims=True
            )
            dpre[rows, cols] = (back * slope[0:wave_rows, cols]).astype(jnp.bfloat16)

        remote(dpre.at[rows], dpre_far.at[rows], dfs_sem.at[w], dfr_sem.at[w], (mate_a, me))
        logit[rows, :] = logit[rows, :] * closed
        arrived(x_send.at[travels(w)], xs_sem.at[w])

        @pl.loop(0, 8)
        def _(n):
            cols = pl.ds(pl.multiple_of(n * 512, 512), 512)
            partial = lax.dot_general(
                dpre[rows, :], w_up[cols, :], TRAIL, preferred_element_type=jnp.float32
            )
            partial = partial + logit[rows, :] * column[:, cols]
            x_send[rows, cols] = partial.astype(jnp.bfloat16)

        return_blocks(w, x_send, r_in, rs_sem, rr_sem)
        if w < N_WAVES - 1:
            add_terms(w)

    def product(left, index, right, left_far, slot, right_far, i, n):
        cols = pl.ds(pl.multiple_of(n * 512, 512), 512)
        offset = i * step_rows
        near = lax.dot_general(
            left[:, columns(index, step_rows, offset)], right[:, cols], ROWS,
            preferred_element_type=jnp.float32,
        )
        other = lax.dot_general(
            left_far[slot, :, pl.ds(offset, step_rows)], right_far[:, cols], ROWS,
            preferred_element_type=jnp.float32,
        )
        return cols, near + other

    def up_piece(i):
        part = pl.ds(i * step_rows, step_rows)

        @pl.loop(0, 2)
        def _(n):
            cols, value = product(x_in, mate_b, dpre, x_far, 1, dpre_far, i, n)
            up_send[part, cols] = value.astype(jnp.bfloat16)

        remote(up_send.at[part], up_got.at[part], ups_sem.at[i], upr_sem.at[i], (mate_b, me))

    def down_piece(i):
        part = pl.ds(i * step_rows, step_rows)

        @pl.loop(0, 2)
        def _(n):
            cols, value = product(g_in, mate_a, act, g_far, 1, act_far, i, n)
            down_send[part, cols] = value.astype(jnp.bfloat16)

        remote(down_send.at[part], down_got.at[part], dns_sem.at[i], dnr_sem.at[i], (mate_a, me))

    for chunks in CHUNKS:
        for start in chunks:
            arrived(g_far.at[:, chunk_rows(start, False)], gfr_sem.at[CHUNK_OF[start]])
    for w in range(N_WAVES):
        arrived(act_far.at[span(w)], afr_sem.at[w])
    down_piece(0)
    add_terms(N_WAVES - 1)
    remote(terms_a.at[0:1], terms_a.at[1:2], ts_sem.at[0], tr_sem.at[0], (mate_a, me))
    for w in range(N_WAVES):
        arrived(x_far.at[:, span(w)], xfr_sem.at[w])
        arrived(dpre_far.at[span(w)], dfr_sem.at[w])
    up_piece(0)
    for i in range(1, PIECES):
        down_piece(i)
        up_piece(i)
        if i == 1:
            arrived(terms_a.at[1:2], tr_sem.at[0])
            terms_b[0:1, :] = terms_a[0:1, :] + terms_a[1:2, :]
            remote(terms_b.at[0:1], terms_b.at[1:2], ts_sem.at[1], tr_sem.at[1], (mate_b, me))

    for i in range(PIECES):
        part = pl.ds(i * step_rows, step_rows)

        @pl.loop(0, 2)
        def _(n):
            cols, value = product(g_in, shard, act, g_far, 0, act_far, i, n)
            own_sum[0, :, cols] = value
            cols, value = product(x_in, shard, dpre, x_far, 0, dpre_far, i, n)
            own_sum[1, :, cols] = value

        if i == PIECES - 1:
            arrived(terms_b.at[1:2], tr_sem.at[1])
            terms_out[...] = terms_b[0:1, :] + terms_b[1:2, :]
            for w in range(N_WAVES):
                arrived(r_in.at[travels(w)], rr_sem.at[w])

            @pl.loop(0, 8)
            def _(n):
                cols = pl.ds(pl.multiple_of(n * 512, 512), 512)
                tokens_grad[:, cols] = jnp.dot(
                    pick_back[...], r_in[:, cols], preferred_element_type=jnp.float32
                ).astype(jnp.bfloat16)

        arrived(down_got.at[part], dnr_sem.at[i])
        down_got[part, :] = (own_sum[0] + down_got[part, :].astype(jnp.float32)).astype(
            jnp.bfloat16
        )
        pltpu.make_async_copy(down_got.at[part], down_out.at[part], out_sem.at[0, i]).start()
        arrived(up_got.at[part], upr_sem.at[i])
        up_got[part, :] = (own_sum[1] + up_got[part, :].astype(jnp.float32)).astype(jnp.bfloat16)
        pltpu.make_async_copy(up_got.at[part], up_out.at[part], out_sem.at[1, i]).start()

    for w in range(N_WAVES):
        arrived(g_send.at[travels(w)], gs_sem.at[w])
        arrived(x_send.at[travels(w)], rs_sem.at[w])
        arrived(x_far.at[:, span(w)], xfs_sem.at[w])
        arrived(act.at[span(w)], afs_sem.at[w])
        arrived(dpre.at[span(w)], dfs_sem.at[w])
    for chunks in CHUNKS:
        for start in chunks:
            arrived(g_far.at[:, chunk_rows(start, False)], gfs_sem.at[CHUNK_OF[start]])
    arrived(terms_a.at[0:1], ts_sem.at[0])
    arrived(terms_b.at[0:1], ts_sem.at[1])
    for i in range(PIECES):
        part = pl.ds(i * step_rows, step_rows)
        arrived(down_send.at[part], dns_sem.at[i])
        arrived(up_send.at[part], ups_sem.at[i])
        pltpu.make_async_copy(down_got.at[part], down_out.at[part], out_sem.at[0, i]).wait()
        pltpu.make_async_copy(up_got.at[part], up_out.at[part], out_sem.at[1, i]).wait()


def on_device(tokens, out_grad, route_slots, expert_counts, router_weight, up_weight, down_weight):
    tok_rows, width = tokens.shape
    hidden = up_weight.shape[2]
    piece = width // 4
    slots = route_slots[0, 0]
    experts, per_slot = slots.shape
    received = experts * per_slot
    slots = slots.reshape(1, received)
    counts = expert_counts.reshape(1, tok_rows)
    router = router_weight.T

    half = jnp.bfloat16
    vmem = pl.BlockSpec(memory_space=pltpu.VMEM)
    anywhere = pl.BlockSpec(memory_space=pl.ANY)
    dma = pltpu.SemaphoreType.DMA
    rows_buffer = pltpu.VMEM((received, width), half)
    inner = pltpu.VMEM((received, hidden), half)
    halves = pltpu.VMEM((2, received, piece), half)
    square = pltpu.VMEM((piece, hidden), half)
    full = pltpu.VMEM((width, hidden), half)
    tokens_grad, up_sum, down_sum, terms = pl.pallas_call(
        kernel,
        out_shape=(
            jax.ShapeDtypeStruct((tok_rows, width), half),
            jax.ShapeDtypeStruct((piece, hidden), half),
            jax.ShapeDtypeStruct((piece, hidden), half),
            jax.ShapeDtypeStruct((1, width), jnp.float32),
        ),
        in_specs=[vmem] * 5 + [anywhere] * 2,
        out_specs=(vmem, anywhere, anywhere, vmem),
        scratch_shapes=[
            pltpu.VMEM((received, tok_rows), half), pltpu.VMEM((tok_rows, received), half),
            pltpu.VMEM((experts, tok_rows), jnp.float32), pltpu.VMEM((1, width), jnp.float32),
            rows_buffer, rows_buffer, rows_buffer, rows_buffer, rows_buffer, full, full,
            inner, pltpu.VMEM((max(COUNTS) * BLOCK, hidden), jnp.float32), inner,
            pltpu.VMEM((received, 1), jnp.float32),
            halves, inner, halves, inner, square, square, square, square,
            pltpu.VMEM((2, piece // PIECES, hidden), jnp.float32),
            pltpu.VMEM((2, width), jnp.float32), pltpu.VMEM((2, width), jnp.float32),
            dma((2,)),
        ]
        + [dma((N_WAVES,))] * 3 + [dma((N_CHUNKS,))] + [dma((N_WAVES,))] * 2
        + [dma((N_WAVES,))] * 4 + [dma((N_CHUNKS,))] * 2 + [dma((N_WAVES,))] * 2
        + [dma((PIECES,))] * 4
        + [dma((2,)), dma((2,)), dma((2, PIECES))],
        compiler_params=pltpu.CompilerParams(
            collective_id=0, has_side_effects=True, vmem_limit_bytes=67043328
        ),
        name="exchange",
    )(tokens, out_grad, slots, counts, router, up_weight[0], down_weight[0])
    return (tokens_grad, up_sum[None], down_sum[None], terms.reshape(width, 1))


def solution(mesh):
    return jax.shard_map(
        on_device,
        mesh=mesh,
        in_specs=(
            P(("dp", "expert"), None),
            P(("dp", "expert"), None),
            P("dp", "expert", None, None),
            P(("dp", "expert")),
            P(),
            P("expert", None, None),
            P("expert", None, None),
        ),
        out_specs=(
            P(("dp", "expert"), None),
            P("expert", "dp", None),
            P("expert", "dp", None),
            P(None, "expert"),
        ),
        check_vma=False,
    )
```

```python
import functools

import jax
import jax.numpy as jnp
from jax import lax
from jax.experimental import pallas as pl
from jax.experimental.pallas import tpu as pltpu
from jax.sharding import PartitionSpec as P

MESH = pl.DeviceIdType.MESH
TRAIL = (((1,), (1,)), ((), ()))
ROWS = (((0,), (0,)), ((), ()))
WAVES = (
    ((0, 0), (2, 2), (2, 0), (0, 2)),
    ((2, 1), (2, 3), (0, 1), (0, 3)),
    ((1, 2), (3, 2), (1, 0), (3, 0)),
    ((1, 1), (3, 3), (1, 3), (3, 1)),
)
STEPS = tuple(
    (dz, dx, dc) if dc == 0 else (-dz % 4, -dx % 4, dc)
    for wave in WAVES
    for dz, dx in wave
    for dc in (0, 1)
)
COUNTS = tuple(2 * len(wave) for wave in WAVES)
FIRST = tuple(sum(COUNTS[:w]) for w in range(len(WAVES)))
SELF = STEPS.index((0, 0, 0))
N_WAVES = len(WAVES)
BLOCK = 16
AHEAD = 2
CHUNKS = tuple(
    tuple(range(first, first + count, count if w < N_WAVES - 1 else 2))
    for w, (first, count) in enumerate(zip(FIRST, COUNTS))
)
CHUNK_OF = tuple(
    sum(1 for chunks in CHUNKS for start in chunks if start <= k) - 1 for k in range(len(STEPS))
)
WAVE_OF = tuple(sum(1 for first in FIRST if first <= k) - 1 for k in range(len(STEPS)))
N_CHUNKS = CHUNK_OF[-1] + 1
PIECES = 4


def shifted(me, step, sign):
    dz, dx, dc = step
    z, x, c = me // 8, (me // 2) % 4, me % 2
    other = (c + dc) % 2
    swap = c if sign > 0 else other
    z = (z + sign * (dz + swap * (dx - dz)) + 4) % 4
    x = (x + sign * (dx + swap * (dz - dx)) + 4) % 4
    return (z * 4 + x) * 2 + other


def gelu_pair(values):
    inner = 0.7978845608 * (values + 0.044715 * values * values * values)
    tangent = jnp.tanh(inner)
    result = 0.5 * values * (1.0 + tangent)
    slope = 0.5 * (1.0 + tangent) + 0.5 * values * (1.0 - tangent * tangent) * 0.7978845608 * (
        1.0 + 3.0 * 0.044715 * values * values
    )
    return (result, slope)


def kernel(
    tokens, grads, slots, counts, router, up_hbm, down_hbm,
    tokens_grad, up_out, down_out, terms_out,
    pick, pick_back, scaled, column,
    x_send, g_send, x_in, g_in, r_in, w_up, w_down, act, slope, dpre, logit,
    x_far, dpre_far, g_far, act_far, up_send, down_send, up_got, down_got, own_sum,
    terms_a, terms_b,
    w_sem, xs_sem, xr_sem, gs_sem, gr_sem, rs_sem, rr_sem,
    xfs_sem, xfr_sem, dfs_sem, dfr_sem, gfs_sem, gfr_sem, afs_sem, afr_sem,
    ups_sem, upr_sem, dns_sem, dnr_sem, ts_sem, tr_sem, out_sem,
):
    shard = lax.axis_index("dp")
    me = lax.axis_index("expert")
    mate_a = shard + 1 - 2 * (shard % 2)
    mate_b = 3 - shard
    far = 3 - mate_a
    width = tokens.shape[1]
    hidden = act.shape[1]
    piece = width // 4
    step_rows = piece // PIECES

    load_up = pltpu.make_async_copy(up_hbm, w_up, w_sem.at[0])
    load_down = pltpu.make_async_copy(down_hbm, w_down, w_sem.at[1])
    load_up.start()
    load_down.start()

    barrier = pltpu.get_barrier_semaphore()
    for step in STEPS:
        if step != (0, 0, 0):
            pl.semaphore_signal(
                barrier, inc=1, device_id=(shard, shifted(me, step, 1)), device_id_type=MESH
            )
    pl.semaphore_signal(barrier, inc=1, device_id=(mate_a, me), device_id_type=MESH)
    pl.semaphore_signal(barrier, inc=1, device_id=(mate_b, me), device_id_type=MESH)

    def span(w):
        return pl.ds(FIRST[w] * BLOCK, COUNTS[w] * BLOCK)

    def columns(index, size=piece, offset=0):
        return pl.ds(pl.multiple_of(index * piece + offset, 128), size)

    def arrived(ref, sem):
        pltpu.make_async_copy(ref, ref, sem).wait()

    def remote(src, dst, send, recv, device):
        copy = pltpu.make_async_remote_copy(
            src_ref=src, dst_ref=dst, send_sem=send, recv_sem=recv,
            device_id=device, device_id_type=MESH,
        )
        copy.start()

    def travels(w):
        if FIRST[w] == SELF:
            return pl.ds((SELF + 1) * BLOCK, (COUNTS[w] - 1) * BLOCK)
        return span(w)

    def chunk_rows(start, traveled):
        count = sum(1 for k in CHUNK_OF if k == CHUNK_OF[start])
        skip = 1 if traveled and start == SELF else 0
        return pl.ds((start + skip) * BLOCK, (count - skip) * BLOCK)

    def send_blocks(w, src, dst, send, recv, tags):
        for k in range(FIRST[w], FIRST[w] + COUNTS[w]):
            rows = pl.ds(k * BLOCK, BLOCK)
            if k == SELF:
                dst[rows, :] = src[rows, :]
            else:
                remote(
                    src.at[rows], dst.at[rows], send.at[w], recv.at[tags[k]],
                    (shard, shifted(me, STEPS[k], 1)),
                )

    def return_blocks(w, src, dst, send, recv):
        for k in range(FIRST[w], FIRST[w] + COUNTS[w]):
            rows = pl.ds(k * BLOCK, BLOCK)
            home = pl.ds(pl.multiple_of(me * BLOCK, BLOCK), BLOCK)
            if k == SELF:
                dst[home, :] = src[rows, :]
            else:
                remote(
                    src.at[rows], dst.at[home], send.at[w], recv.at[w],
                    (shard, shifted(me, STEPS[k], -1)),
                )

    def add_terms(w):
        rows = span(w)
        for n in range(8):
            cols = pl.ds(n * 512, 512)
            value = jnp.sum(
                x_in[rows, cols].astype(jnp.float32) * logit[rows, :], axis=0, keepdims=True
            )
            terms_a[0:1, cols] = value if w == 0 else terms_a[0:1, cols] + value

    def give_back(w):
        rows = span(w)
        arrived(x_send.at[travels(w)], xs_sem.at[w])

        @pl.loop(0, 8)
        def _(n):
            cols = pl.ds(pl.multiple_of(n * 512, 512), 512)
            partial = lax.dot_general(
                dpre[rows, :], w_up[cols, :], TRAIL, preferred_element_type=jnp.float32
            )
            partial = partial + logit[rows, :] * column[:, cols]
            x_send[rows, cols] = partial.astype(jnp.bfloat16)

    def wave_steps(w):
        return [shifted(me, STEPS[k], 1) for k in range(FIRST[w], FIRST[w] + COUNTS[w])]

    def wave_picks(w):
        return [pick[pl.ds(pl.multiple_of(to * BLOCK, BLOCK), BLOCK), :] for to in wave_steps(w)]

    def select_tokens(w):
        chosen = jnp.concatenate(wave_picks(w), axis=0)

        @pl.loop(0, 4)
        def _(n):
            cols = columns(n)
            picked = jnp.dot(chosen, tokens[:, cols], preferred_element_type=jnp.float32)
            x_send[span(w), cols] = picked.astype(jnp.bfloat16)

    def select_grads(w):
        picks = wave_picks(w)
        chosen = jnp.concatenate(picks, axis=0)
        weight = jnp.concatenate(
            [
                jnp.sum(one.astype(jnp.float32) * scaled[pl.ds(to, 1), :], axis=1, keepdims=True)
                for one, to in zip(picks, wave_steps(w))
            ],
            axis=0,
        )

        @pl.loop(0, 4)
        def _(n):
            cols = columns(n)
            picked = jnp.dot(chosen, grads[:, cols], preferred_element_type=jnp.float32)
            g_send[span(w), cols] = (weight * picked).astype(jnp.bfloat16)

    tok_rows = tokens.shape[0]
    places = lax.broadcasted_iota(jnp.int32, (tok_rows, slots.shape[1]), 0)
    hits = jnp.where(places == slots[...], 1.0, 0.0)
    pick_back[...] = hits.astype(jnp.bfloat16)
    pick[...] = hits.T.astype(jnp.bfloat16)
    select_tokens(0)
    pl.semaphore_wait(barrier, len(STEPS) + 1)
    send_blocks(0, x_send, x_in, xs_sem, xr_sem, WAVE_OF)

    logits = jnp.zeros((router.shape[0], tok_rows), jnp.float32)
    rest = router[...]
    for _ in range(3):
        head = rest.astype(jnp.bfloat16)
        rest = rest - head.astype(jnp.float32)
        logits = logits + lax.dot_general(
            head, tokens[...], TRAIL, preferred_element_type=jnp.float32
        )
    tallies = jnp.maximum(counts[...], 1).astype(jnp.float32)
    scaled[...] = jax.nn.sigmoid(logits) / tallies
    column[...] = router[pl.ds(me, 1), :]
    def send_tokens(w):
        select_tokens(w)
        send_blocks(w, x_send, x_in, xs_sem, xr_sem, WAVE_OF)

    def send_grads(w):
        select_grads(w)
        send_blocks(w, g_send, g_in, gs_sem, gr_sem, CHUNK_OF)

    send_grads(0)
    for w in range(1, AHEAD):
        send_tokens(w)
        send_grads(w)

    load_up.wait()
    load_down.wait()
    for w in range(N_WAVES):
        rows = span(w)
        wave_rows = COUNTS[w] * BLOCK
        arrived(x_in.at[travels(w)], xr_sem.at[w])
        if w + AHEAD < N_WAVES:
            send_tokens(w + AHEAD)
        for slot, index in ((1, far), (0, mate_a)):
            remote(
                x_in.at[rows, columns(index)], x_far.at[slot, rows],
                xfs_sem.at[w], xfr_sem.at[w], (mate_a, me),
            )

        @pl.loop(0, 4)
        def _(n):
            cols = pl.ds(pl.multiple_of(n * 256, 256), 256)
            pre = jnp.dot(x_in[rows, :], w_up[:, cols], preferred_element_type=jnp.float32)
            active, bend = gelu_pair(pre)
            act[rows, cols] = active.astype(jnp.bfloat16)
            slope[0:wave_rows, cols] = bend

        remote(act.at[rows], act_far.at[rows], afs_sem.at[w], afr_sem.at[w], (mate_b, me))
        gate = jnp.zeros((wave_rows, 1), jnp.float32)
        for n in range(4):
            cols = pl.ds(n * piece, piece)
            gate = gate + jnp.sum(
                x_in[rows, cols].astype(jnp.float32) * column[:, cols], axis=1, keepdims=True
            )
        closed = 1.0 - jax.nn.sigmoid(gate)
        for start in CHUNKS[w]:
            tag = CHUNK_OF[start]
            arrived(g_in.at[chunk_rows(start, True)], gr_sem.at[tag])
            some = chunk_rows(start, False)
            for slot, index in ((1, far), (0, mate_b)):
                remote(
                    g_in.at[some, columns(index)], g_far.at[slot, some],
                    gfs_sem.at[tag], gfr_sem.at[tag], (mate_b, me),
                )
        if w + AHEAD < N_WAVES:
            send_grads(w + AHEAD)
            if w + AHEAD == N_WAVES - 1:
                for early in range(w):
                    return_blocks(early, x_send, r_in, rs_sem, rr_sem)
        logit[rows, :] = jnp.zeros((wave_rows, 1), jnp.float32)

        @pl.loop(0, 4)
        def _(n):
            cols = pl.ds(pl.multiple_of(n * 256, 256), 256)
            back = jnp.dot(g_in[rows, :], w_down[:, cols], preferred_element_type=jnp.float32)
            logit[rows, :] += jnp.sum(
                act[rows, cols].astype(jnp.float32) * back, axis=1, keepdims=True
            )
            dpre[rows, cols] = (back * slope[0:wave_rows, cols]).astype(jnp.bfloat16)

        remote(dpre.at[rows], dpre_far.at[rows], dfs_sem.at[w], dfr_sem.at[w], (mate_a, me))
        logit[rows, :] = logit[rows, :] * closed
        give_back(w)
        if w + AHEAD >= N_WAVES - 1:
            return_blocks(w, x_send, r_in, rs_sem, rr_sem)
        if w < N_WAVES - 1:
            add_terms(w)

    def product(left, index, right, left_far, slot, right_far, i, n):
        cols = pl.ds(pl.multiple_of(n * 512, 512), 512)
        offset = i * step_rows
        near = lax.dot_general(
            left[:, columns(index, step_rows, offset)], right[:, cols], ROWS,
            preferred_element_type=jnp.float32,
        )
        other = lax.dot_general(
            left_far[slot, :, pl.ds(offset, step_rows)], right_far[:, cols], ROWS,
            preferred_element_type=jnp.float32,
        )
        return cols, near + other

    def up_piece(i):
        part = pl.ds(i * step_rows, step_rows)

        @pl.loop(0, 2)
        def _(n):
            cols, value = product(x_in, mate_b, dpre, x_far, 1, dpre_far, i, n)
            up_send[part, cols] = value.astype(jnp.bfloat16)

        remote(up_send.at[part], up_got.at[part], ups_sem.at[i], upr_sem.at[i], (mate_b, me))

    def down_piece(i):
        part = pl.ds(i * step_rows, step_rows)

        @pl.loop(0, 2)
        def _(n):
            cols, value = product(g_in, mate_a, act, g_far, 1, act_far, i, n)
            down_send[part, cols] = value.astype(jnp.bfloat16)

        remote(down_send.at[part], down_got.at[part], dns_sem.at[i], dnr_sem.at[i], (mate_a, me))

    for chunks in CHUNKS:
        for start in chunks:
            arrived(g_far.at[:, chunk_rows(start, False)], gfr_sem.at[CHUNK_OF[start]])
    for w in range(N_WAVES):
        arrived(act_far.at[span(w)], afr_sem.at[w])
    down_piece(0)
    add_terms(N_WAVES - 1)
    remote(terms_a.at[0:1], terms_a.at[1:2], ts_sem.at[0], tr_sem.at[0], (mate_a, me))
    for w in range(N_WAVES):
        arrived(x_far.at[:, span(w)], xfr_sem.at[w])
        arrived(dpre_far.at[span(w)], dfr_sem.at[w])
    up_piece(0)
    for i in range(1, PIECES):
        down_piece(i)
        up_piece(i)
        if i == 1:
            arrived(terms_a.at[1:2], tr_sem.at[0])
            terms_b[0:1, :] = terms_a[0:1, :] + terms_a[1:2, :]
            remote(terms_b.at[0:1], terms_b.at[1:2], ts_sem.at[1], tr_sem.at[1], (mate_b, me))

    for i in range(PIECES):
        part = pl.ds(i * step_rows, step_rows)

        @pl.loop(0, 2)
        def _(n):
            cols, value = product(g_in, shard, act, g_far, 0, act_far, i, n)
            own_sum[0, :, cols] = value
            cols, value = product(x_in, shard, dpre, x_far, 0, dpre_far, i, n)
            own_sum[1, :, cols] = value

        if i == PIECES - 1:
            arrived(terms_b.at[1:2], tr_sem.at[1])
            terms_out[...] = terms_b[0:1, :] + terms_b[1:2, :]
            for w in range(N_WAVES):
                arrived(r_in.at[travels(w)], rr_sem.at[w])

            @pl.loop(0, 8)
            def _(n):
                cols = pl.ds(pl.multiple_of(n * 512, 512), 512)
                tokens_grad[:, cols] = jnp.dot(
                    pick_back[...], r_in[:, cols], preferred_element_type=jnp.float32
                ).astype(jnp.bfloat16)

        arrived(down_got.at[part], dnr_sem.at[i])
        down_got[part, :] = (own_sum[0] + down_got[part, :].astype(jnp.float32)).astype(
            jnp.bfloat16
        )
        pltpu.make_async_copy(down_got.at[part], down_out.at[part], out_sem.at[0, i]).start()
        arrived(up_got.at[part], upr_sem.at[i])
        up_got[part, :] = (own_sum[1] + up_got[part, :].astype(jnp.float32)).astype(jnp.bfloat16)
        pltpu.make_async_copy(up_got.at[part], up_out.at[part], out_sem.at[1, i]).start()

    for w in range(N_WAVES):
        arrived(g_send.at[travels(w)], gs_sem.at[w])
        arrived(x_send.at[travels(w)], rs_sem.at[w])
        arrived(x_far.at[:, span(w)], xfs_sem.at[w])
        arrived(act.at[span(w)], afs_sem.at[w])
        arrived(dpre.at[span(w)], dfs_sem.at[w])
    for chunks in CHUNKS:
        for start in chunks:
            arrived(g_far.at[:, chunk_rows(start, False)], gfs_sem.at[CHUNK_OF[start]])
    arrived(terms_a.at[0:1], ts_sem.at[0])
    arrived(terms_b.at[0:1], ts_sem.at[1])
    for i in range(PIECES):
        part = pl.ds(i * step_rows, step_rows)
        arrived(down_send.at[part], dns_sem.at[i])
        arrived(up_send.at[part], ups_sem.at[i])
        pltpu.make_async_copy(down_got.at[part], down_out.at[part], out_sem.at[0, i]).wait()
        pltpu.make_async_copy(up_got.at[part], up_out.at[part], out_sem.at[1, i]).wait()


def on_device(tokens, out_grad, route_slots, expert_counts, router_weight, up_weight, down_weight):
    tok_rows, width = tokens.shape
    hidden = up_weight.shape[2]
    piece = width // 4
    slots = route_slots[0, 0]
    experts, per_slot = slots.shape
    received = experts * per_slot
    slots = slots.reshape(1, received)
    counts = expert_counts.reshape(1, tok_rows)
    router = router_weight.T

    half = jnp.bfloat16
    vmem = pl.BlockSpec(memory_space=pltpu.VMEM)
    anywhere = pl.BlockSpec(memory_space=pl.ANY)
    dma = pltpu.SemaphoreType.DMA
    rows_buffer = pltpu.VMEM((received, width), half)
    inner = pltpu.VMEM((received, hidden), half)
    halves = pltpu.VMEM((2, received, piece), half)
    square = pltpu.VMEM((piece, hidden), half)
    full = pltpu.VMEM((width, hidden), half)
    tokens_grad, up_sum, down_sum, terms = pl.pallas_call(
        kernel,
        out_shape=(
            jax.ShapeDtypeStruct((tok_rows, width), half),
            jax.ShapeDtypeStruct((piece, hidden), half),
            jax.ShapeDtypeStruct((piece, hidden), half),
            jax.ShapeDtypeStruct((1, width), jnp.float32),
        ),
        in_specs=[vmem] * 5 + [anywhere] * 2,
        out_specs=(vmem, anywhere, anywhere, vmem),
        scratch_shapes=[
            pltpu.VMEM((received, tok_rows), half), pltpu.VMEM((tok_rows, received), half),
            pltpu.VMEM((experts, tok_rows), jnp.float32), pltpu.VMEM((1, width), jnp.float32),
            rows_buffer, rows_buffer, rows_buffer, rows_buffer, rows_buffer, full, full,
            inner, pltpu.VMEM((max(COUNTS) * BLOCK, hidden), jnp.float32), inner,
            pltpu.VMEM((received, 1), jnp.float32),
            halves, inner, halves, inner, square, square, square, square,
            pltpu.VMEM((2, piece // PIECES, hidden), jnp.float32),
            pltpu.VMEM((2, width), jnp.float32), pltpu.VMEM((2, width), jnp.float32),
            dma((2,)),
        ]
        + [dma((N_WAVES,))] * 3 + [dma((N_CHUNKS,))] + [dma((N_WAVES,))] * 2
        + [dma((N_WAVES,))] * 4 + [dma((N_CHUNKS,))] * 2 + [dma((N_WAVES,))] * 2
        + [dma((PIECES,))] * 4
        + [dma((2,)), dma((2,)), dma((2, PIECES))],
        compiler_params=pltpu.CompilerParams(
            collective_id=0, has_side_effects=True, vmem_limit_bytes=67043328
        ),
        name="exchange",
    )(tokens, out_grad, slots, counts, router, up_weight[0], down_weight[0])
    return (tokens_grad, up_sum[None], down_sum[None], terms.reshape(width, 1))


def solution(mesh):
    return jax.shard_map(
        on_device,
        mesh=mesh,
        in_specs=(
            P(("dp", "expert"), None),
            P(("dp", "expert"), None),
            P("dp", "expert", None, None),
            P(("dp", "expert")),
            P(),
            P("expert", None, None),
            P("expert", None, None),
        ),
        out_specs=(
            P(("dp", "expert"), None),
            P("expert", "dp", None),
            P("expert", "dp", None),
            P(None, "expert"),
        ),
        check_vma=False,
    )
```

```python
import functools

import jax
import jax.numpy as jnp
from jax import lax
from jax.experimental import pallas as pl
from jax.experimental.pallas import tpu as pltpu
from jax.sharding import PartitionSpec as P

MESH = pl.DeviceIdType.MESH
TRAIL = (((1,), (1,)), ((), ()))
ROWS = (((0,), (0,)), ((), ()))
WAVES = (
    ((0, 0), (2, 2), (2, 0), (0, 2)),
    ((2, 1), (2, 3), (0, 1), (0, 3)),
    ((1, 2), (3, 2), (1, 0), (3, 0)),
    ((1, 1), (3, 3), (1, 3), (3, 1)),
)
STEPS = tuple(
    (dz, dx, dc) if dc == 0 else (-dz % 4, -dx % 4, dc)
    for wave in WAVES
    for dz, dx in wave
    for dc in (0, 1)
)
COUNTS = tuple(2 * len(wave) for wave in WAVES)
FIRST = tuple(sum(COUNTS[:w]) for w in range(len(WAVES)))
SELF = STEPS.index((0, 0, 0))
N_WAVES = len(WAVES)
BLOCK = 16
AHEAD = 2
CHUNKS = tuple(
    tuple(range(first, first + count, count if w < N_WAVES - 1 else count // 2))
    for w, (first, count) in enumerate(zip(FIRST, COUNTS))
)
CHUNK_OF = tuple(
    sum(1 for chunks in CHUNKS for start in chunks if start <= k) - 1 for k in range(len(STEPS))
)
WAVE_OF = tuple(sum(1 for first in FIRST if first <= k) - 1 for k in range(len(STEPS)))
N_CHUNKS = CHUNK_OF[-1] + 1
PIECES = 4


def shifted(me, step, sign):
    dz, dx, dc = step
    z, x, c = me // 8, (me // 2) % 4, me % 2
    other = (c + dc) % 2
    swap = c if sign > 0 else other
    z = (z + sign * (dz + swap * (dx - dz)) + 4) % 4
    x = (x + sign * (dx + swap * (dz - dx)) + 4) % 4
    return (z * 4 + x) * 2 + other


def gelu_pair(values):
    inner = 0.7978845608 * (values + 0.044715 * values * values * values)
    tangent = jnp.tanh(inner)
    result = 0.5 * values * (1.0 + tangent)
    slope = 0.5 * (1.0 + tangent) + 0.5 * values * (1.0 - tangent * tangent) * 0.7978845608 * (
        1.0 + 3.0 * 0.044715 * values * values
    )
    return (result, slope)


def kernel(
    tokens, grads, slots, counts, router, up_hbm, down_hbm,
    tokens_grad, up_out, down_out, terms_out,
    pick, pick_back, scaled, column,
    x_send, g_send, x_in, g_in, r_in, w_up, w_down, act, slope, dpre, logit,
    x_far, dpre_far, g_far, act_far, up_send, down_send, up_got, down_got, own_sum,
    terms_a, terms_b,
    w_sem, xs_sem, xr_sem, gs_sem, gr_sem, rs_sem, rr_sem,
    xfs_sem, xfr_sem, dfs_sem, dfr_sem, gfs_sem, gfr_sem, afs_sem, afr_sem,
    ups_sem, upr_sem, dns_sem, dnr_sem, ts_sem, tr_sem, out_sem,
):
    shard = lax.axis_index("dp")
    me = lax.axis_index("expert")
    mate_a = shard + 1 - 2 * (shard % 2)
    mate_b = 3 - shard
    far = 3 - mate_a
    width = tokens.shape[1]
    hidden = act.shape[1]
    piece = width // 4
    step_rows = piece // PIECES

    load_up = pltpu.make_async_copy(up_hbm, w_up, w_sem.at[0])
    load_down = pltpu.make_async_copy(down_hbm, w_down, w_sem.at[1])
    load_up.start()
    load_down.start()

    barrier = pltpu.get_barrier_semaphore()
    for step in STEPS:
        if step != (0, 0, 0):
            pl.semaphore_signal(
                barrier, inc=1, device_id=(shard, shifted(me, step, 1)), device_id_type=MESH
            )
    pl.semaphore_signal(barrier, inc=1, device_id=(mate_a, me), device_id_type=MESH)
    pl.semaphore_signal(barrier, inc=1, device_id=(mate_b, me), device_id_type=MESH)

    def span(w):
        return pl.ds(FIRST[w] * BLOCK, COUNTS[w] * BLOCK)

    def columns(index, size=piece, offset=0):
        return pl.ds(pl.multiple_of(index * piece + offset, 128), size)

    def arrived(ref, sem):
        pltpu.make_async_copy(ref, ref, sem).wait()

    def remote(src, dst, send, recv, device):
        copy = pltpu.make_async_remote_copy(
            src_ref=src, dst_ref=dst, send_sem=send, recv_sem=recv,
            device_id=device, device_id_type=MESH,
        )
        copy.start()

    def travels(w):
        if FIRST[w] == SELF:
            return pl.ds((SELF + 1) * BLOCK, (COUNTS[w] - 1) * BLOCK)
        return span(w)

    def chunk_rows(start, traveled):
        count = sum(1 for k in CHUNK_OF if k == CHUNK_OF[start])
        skip = 1 if traveled and start == SELF else 0
        return pl.ds((start + skip) * BLOCK, (count - skip) * BLOCK)

    def send_blocks(w, src, dst, send, recv, tags):
        for k in range(FIRST[w], FIRST[w] + COUNTS[w]):
            rows = pl.ds(k * BLOCK, BLOCK)
            if k == SELF:
                dst[rows, :] = src[rows, :]
            else:
                remote(
                    src.at[rows], dst.at[rows], send.at[w], recv.at[tags[k]],
                    (shard, shifted(me, STEPS[k], 1)),
                )

    def return_blocks(w, src, dst, send, recv):
        for k in range(FIRST[w], FIRST[w] + COUNTS[w]):
            rows = pl.ds(k * BLOCK, BLOCK)
            home = pl.ds(pl.multiple_of(me * BLOCK, BLOCK), BLOCK)
            if k == SELF:
                dst[home, :] = src[rows, :]
            else:
                remote(
                    src.at[rows], dst.at[home], send.at[w], recv.at[w],
                    (shard, shifted(me, STEPS[k], -1)),
                )

    def add_terms(w):
        rows = span(w)
        for n in range(8):
            cols = pl.ds(n * 512, 512)
            value = jnp.sum(
                x_in[rows, cols].astype(jnp.float32) * logit[rows, :], axis=0, keepdims=True
            )
            terms_a[0:1, cols] = value if w == 0 else terms_a[0:1, cols] + value

    def give_back(w):
        rows = span(w)
        arrived(x_send.at[travels(w)], xs_sem.at[w])

        @pl.loop(0, 8)
        def _(n):
            cols = pl.ds(pl.multiple_of(n * 512, 512), 512)
            partial = lax.dot_general(
                dpre[rows, :], w_up[cols, :], TRAIL, preferred_element_type=jnp.float32
            )
            partial = partial + logit[rows, :] * column[:, cols]
            x_send[rows, cols] = partial.astype(jnp.bfloat16)

    def wave_steps(w):
        return [shifted(me, STEPS[k], 1) for k in range(FIRST[w], FIRST[w] + COUNTS[w])]

    def wave_picks(w):
        return [pick[pl.ds(pl.multiple_of(to * BLOCK, BLOCK), BLOCK), :] for to in wave_steps(w)]

    def select_tokens(w):
        chosen = jnp.concatenate(wave_picks(w), axis=0)

        @pl.loop(0, 4)
        def _(n):
            cols = columns(n)
            picked = jnp.dot(chosen, tokens[:, cols], preferred_element_type=jnp.float32)
            x_send[span(w), cols] = picked.astype(jnp.bfloat16)

    def select_grads(w):
        picks = wave_picks(w)
        chosen = jnp.concatenate(picks, axis=0)
        weight = jnp.concatenate(
            [
                jnp.sum(one.astype(jnp.float32) * scaled[pl.ds(to, 1), :], axis=1, keepdims=True)
                for one, to in zip(picks, wave_steps(w))
            ],
            axis=0,
        )

        @pl.loop(0, 4)
        def _(n):
            cols = columns(n)
            picked = jnp.dot(chosen, grads[:, cols], preferred_element_type=jnp.float32)
            g_send[span(w), cols] = (weight * picked).astype(jnp.bfloat16)

    tok_rows = tokens.shape[0]
    places = lax.broadcasted_iota(jnp.int32, (tok_rows, slots.shape[1]), 0)
    hits = jnp.where(places == slots[...], 1.0, 0.0)
    pick_back[...] = hits.astype(jnp.bfloat16)
    pick[...] = hits.T.astype(jnp.bfloat16)
    select_tokens(0)
    pl.semaphore_wait(barrier, len(STEPS) + 1)
    send_blocks(0, x_send, x_in, xs_sem, xr_sem, WAVE_OF)

    logits = jnp.zeros((router.shape[0], tok_rows), jnp.float32)
    rest = router[...]
    for _ in range(3):
        head = rest.astype(jnp.bfloat16)
        rest = rest - head.astype(jnp.float32)
        logits = logits + lax.dot_general(
            head, tokens[...], TRAIL, preferred_element_type=jnp.float32
        )
    tallies = jnp.maximum(counts[...], 1).astype(jnp.float32)
    scaled[...] = jax.nn.sigmoid(logits) / tallies
    column[...] = router[pl.ds(me, 1), :]
    def send_tokens(w):
        select_tokens(w)
        send_blocks(w, x_send, x_in, xs_sem, xr_sem, WAVE_OF)

    def send_grads(w):
        select_grads(w)
        send_blocks(w, g_send, g_in, gs_sem, gr_sem, CHUNK_OF)

    send_grads(0)
    for w in range(1, AHEAD):
        send_tokens(w)
        send_grads(w)

    load_up.wait()
    load_down.wait()
    for w in range(N_WAVES):
        rows = span(w)
        wave_rows = COUNTS[w] * BLOCK
        arrived(x_in.at[travels(w)], xr_sem.at[w])
        if w + AHEAD < N_WAVES:
            send_tokens(w + AHEAD)
        for slot, index in ((1, far), (0, mate_a)):
            remote(
                x_in.at[rows, columns(index)], x_far.at[slot, rows],
                xfs_sem.at[w], xfr_sem.at[w], (mate_a, me),
            )

        @pl.loop(0, 4)
        def _(n):
            cols = pl.ds(pl.multiple_of(n * 256, 256), 256)
            pre = jnp.dot(x_in[rows, :], w_up[:, cols], preferred_element_type=jnp.float32)
            active, bend = gelu_pair(pre)
            act[rows, cols] = active.astype(jnp.bfloat16)
            slope[0:wave_rows, cols] = bend

        remote(act.at[rows], act_far.at[rows], afs_sem.at[w], afr_sem.at[w], (mate_b, me))
        gate = jnp.zeros((wave_rows, 1), jnp.float32)
        for n in range(4):
            cols = pl.ds(n * piece, piece)
            gate = gate + jnp.sum(
                x_in[rows, cols].astype(jnp.float32) * column[:, cols], axis=1, keepdims=True
            )
        closed = 1.0 - jax.nn.sigmoid(gate)
        for start in CHUNKS[w]:
            tag = CHUNK_OF[start]
            arrived(g_in.at[chunk_rows(start, True)], gr_sem.at[tag])
            some = chunk_rows(start, False)
            for slot, index in ((1, far), (0, mate_b)):
                remote(
                    g_in.at[some, columns(index)], g_far.at[slot, some],
                    gfs_sem.at[tag], gfr_sem.at[tag], (mate_b, me),
                )
        if w + AHEAD < N_WAVES:
            send_grads(w + AHEAD)
            if w + AHEAD == N_WAVES - 1:
                for early in range(w):
                    return_blocks(early, x_send, r_in, rs_sem, rr_sem)
        logit[rows, :] = jnp.zeros((wave_rows, 1), jnp.float32)

        @pl.loop(0, 4)
        def _(n):
            cols = pl.ds(pl.multiple_of(n * 256, 256), 256)
            back = jnp.dot(g_in[rows, :], w_down[:, cols], preferred_element_type=jnp.float32)
            logit[rows, :] += jnp.sum(
                act[rows, cols].astype(jnp.float32) * back, axis=1, keepdims=True
            )
            dpre[rows, cols] = (back * slope[0:wave_rows, cols]).astype(jnp.bfloat16)

        remote(dpre.at[rows], dpre_far.at[rows], dfs_sem.at[w], dfr_sem.at[w], (mate_a, me))
        logit[rows, :] = logit[rows, :] * closed
        give_back(w)
        if w + AHEAD >= N_WAVES - 1:
            return_blocks(w, x_send, r_in, rs_sem, rr_sem)
        if w < N_WAVES - 1:
            add_terms(w)

    def product(left, index, right, left_far, slot, right_far, i, n):
        cols = pl.ds(pl.multiple_of(n * 512, 512), 512)
        offset = i * step_rows
        near = lax.dot_general(
            left[:, columns(index, step_rows, offset)], right[:, cols], ROWS,
            preferred_element_type=jnp.float32,
        )
        other = lax.dot_general(
            left_far[slot, :, pl.ds(offset, step_rows)], right_far[:, cols], ROWS,
            preferred_element_type=jnp.float32,
        )
        return cols, near + other

    def up_piece(i):
        part = pl.ds(i * step_rows, step_rows)

        @pl.loop(0, 2)
        def _(n):
            cols, value = product(x_in, mate_b, dpre, x_far, 1, dpre_far, i, n)
            up_send[part, cols] = value.astype(jnp.bfloat16)

        remote(up_send.at[part], up_got.at[part], ups_sem.at[i], upr_sem.at[i], (mate_b, me))

    def down_piece(i):
        part = pl.ds(i * step_rows, step_rows)

        @pl.loop(0, 2)
        def _(n):
            cols, value = product(g_in, mate_a, act, g_far, 1, act_far, i, n)
            down_send[part, cols] = value.astype(jnp.bfloat16)

        remote(down_send.at[part], down_got.at[part], dns_sem.at[i], dnr_sem.at[i], (mate_a, me))

    for chunks in CHUNKS:
        for start in chunks:
            arrived(g_far.at[:, chunk_rows(start, False)], gfr_sem.at[CHUNK_OF[start]])
    for w in range(N_WAVES):
        arrived(act_far.at[span(w)], afr_sem.at[w])
    down_piece(0)
    add_terms(N_WAVES - 1)
    remote(terms_a.at[0:1], terms_a.at[1:2], ts_sem.at[0], tr_sem.at[0], (mate_a, me))
    for w in range(N_WAVES):
        arrived(x_far.at[:, span(w)], xfr_sem.at[w])
        arrived(dpre_far.at[span(w)], dfr_sem.at[w])
    up_piece(0)
    for i in range(1, PIECES):
        down_piece(i)
        up_piece(i)
        if i == 1:
            arrived(terms_a.at[1:2], tr_sem.at[0])
            terms_b[0:1, :] = terms_a[0:1, :] + terms_a[1:2, :]
            remote(terms_b.at[0:1], terms_b.at[1:2], ts_sem.at[1], tr_sem.at[1], (mate_b, me))

    for i in range(PIECES):
        part = pl.ds(i * step_rows, step_rows)

        @pl.loop(0, 2)
        def _(n):
            cols, value = product(g_in, shard, act, g_far, 0, act_far, i, n)
            own_sum[0, :, cols] = value
            cols, value = product(x_in, shard, dpre, x_far, 0, dpre_far, i, n)
            own_sum[1, :, cols] = value

        if i == PIECES - 1:
            arrived(terms_b.at[1:2], tr_sem.at[1])
            terms_out[...] = terms_b[0:1, :] + terms_b[1:2, :]
            for w in range(N_WAVES):
                arrived(r_in.at[travels(w)], rr_sem.at[w])

            @pl.loop(0, 8)
            def _(n):
                cols = pl.ds(pl.multiple_of(n * 512, 512), 512)
                tokens_grad[:, cols] = jnp.dot(
                    pick_back[...], r_in[:, cols], preferred_element_type=jnp.float32
                ).astype(jnp.bfloat16)

        arrived(down_got.at[part], dnr_sem.at[i])
        down_got[part, :] = (own_sum[0] + down_got[part, :].astype(jnp.float32)).astype(
            jnp.bfloat16
        )
        pltpu.make_async_copy(down_got.at[part], down_out.at[part], out_sem.at[0, i]).start()
        arrived(up_got.at[part], upr_sem.at[i])
        up_got[part, :] = (own_sum[1] + up_got[part, :].astype(jnp.float32)).astype(jnp.bfloat16)
        pltpu.make_async_copy(up_got.at[part], up_out.at[part], out_sem.at[1, i]).start()

    for w in range(N_WAVES):
        arrived(g_send.at[travels(w)], gs_sem.at[w])
        arrived(x_send.at[travels(w)], rs_sem.at[w])
        arrived(x_far.at[:, span(w)], xfs_sem.at[w])
        arrived(act.at[span(w)], afs_sem.at[w])
        arrived(dpre.at[span(w)], dfs_sem.at[w])
    for chunks in CHUNKS:
        for start in chunks:
            arrived(g_far.at[:, chunk_rows(start, False)], gfs_sem.at[CHUNK_OF[start]])
    arrived(terms_a.at[0:1], ts_sem.at[0])
    arrived(terms_b.at[0:1], ts_sem.at[1])
    for i in range(PIECES):
        part = pl.ds(i * step_rows, step_rows)
        arrived(down_send.at[part], dns_sem.at[i])
        arrived(up_send.at[part], ups_sem.at[i])
        pltpu.make_async_copy(down_got.at[part], down_out.at[part], out_sem.at[0, i]).wait()
        pltpu.make_async_copy(up_got.at[part], up_out.at[part], out_sem.at[1, i]).wait()


def hand_over(first, second, third, first_out, second_out, third_out, a, b, c, in_sem, sem):
    moves = []
    for n, (src, mid, dst) in enumerate(
        ((first, a, first_out), (second, b, second_out), (third, c, third_out))
    ):
        rows = src.shape[0] // 4
        for i in range(4):
            part = pl.ds(i * rows, rows)
            load = pltpu.make_async_copy(src.at[part], mid.at[part], in_sem.at[n, i])
            load.start()
            moves.append((load, mid.at[part], dst.at[part], sem.at[n, i]))
    stores = []
    for load, mid, dst, one in moves:
        load.wait()
        store = pltpu.make_async_copy(mid, dst, one)
        store.start()
        stores.append(store)
    for store in stores:
        store.wait()


def on_device(tokens, out_grad, route_slots, expert_counts, router_weight, up_weight, down_weight):
    tok_rows, width = tokens.shape
    hidden = up_weight.shape[2]
    piece = width // 4
    slots = route_slots[0, 0]
    experts, per_slot = slots.shape
    received = experts * per_slot
    slots = slots.reshape(1, received)
    counts = expert_counts.reshape(1, tok_rows)
    router = router_weight.T

    half = jnp.bfloat16
    vmem = pl.BlockSpec(memory_space=pltpu.VMEM)
    anywhere = pl.BlockSpec(memory_space=pl.ANY)
    dma = pltpu.SemaphoreType.DMA
    rows_buffer = pltpu.VMEM((received, width), half)
    inner = pltpu.VMEM((received, hidden), half)
    halves = pltpu.VMEM((2, received, piece), half)
    square = pltpu.VMEM((piece, hidden), half)
    full = pltpu.VMEM((width, hidden), half)
    tokens_grad, up_sum, down_sum, terms = pl.pallas_call(
        kernel,
        out_shape=(
            jax.ShapeDtypeStruct((tok_rows, width), half),
            jax.ShapeDtypeStruct((piece, hidden), half),
            jax.ShapeDtypeStruct((piece, hidden), half),
            jax.ShapeDtypeStruct((1, width), jnp.float32),
        ),
        in_specs=[vmem] * 5 + [anywhere] * 2,
        out_specs=(vmem, anywhere, anywhere, vmem),
        scratch_shapes=[
            pltpu.VMEM((received, tok_rows), half), pltpu.VMEM((tok_rows, received), half),
            pltpu.VMEM((experts, tok_rows), jnp.float32), pltpu.VMEM((1, width), jnp.float32),
            rows_buffer, rows_buffer, rows_buffer, rows_buffer, rows_buffer, full, full,
            inner, pltpu.VMEM((max(COUNTS) * BLOCK, hidden), jnp.float32), inner,
            pltpu.VMEM((received, 1), jnp.float32),
            halves, inner, halves, inner, square, square, square, square,
            pltpu.VMEM((2, piece // PIECES, hidden), jnp.float32),
            pltpu.VMEM((2, width), jnp.float32), pltpu.VMEM((2, width), jnp.float32),
            dma((2,)),
        ]
        + [dma((N_WAVES,))] * 3 + [dma((N_CHUNKS,))] + [dma((N_WAVES,))] * 2
        + [dma((N_WAVES,))] * 4 + [dma((N_CHUNKS,))] * 2 + [dma((N_WAVES,))] * 2
        + [dma((PIECES,))] * 4
        + [dma((2,)), dma((2,)), dma((2, PIECES))],
        compiler_params=pltpu.CompilerParams(
            collective_id=0, has_side_effects=True, vmem_limit_bytes=67043328
        ),
        name="exchange",
    )(tokens, out_grad, slots, counts, router, up_weight[0], down_weight[0])
    results = (tokens_grad, up_sum, down_sum)
    tokens_grad, up_sum, down_sum = pl.pallas_call(
        hand_over,
        out_shape=tuple(jax.ShapeDtypeStruct(one.shape, one.dtype) for one in results),
        in_specs=[anywhere] * 3,
        out_specs=(anywhere,) * 3,
        scratch_shapes=[pltpu.VMEM(one.shape, one.dtype) for one in results]
        + [dma((3, 4)), dma((3, 4))],
        name="hand_over",
    )(*results)
    return (tokens_grad, up_sum[None], down_sum[None], terms.reshape(width, 1))


def solution(mesh):
    return jax.shard_map(
        on_device,
        mesh=mesh,
        in_specs=(
            P(("dp", "expert"), None),
            P(("dp", "expert"), None),
            P("dp", "expert", None, None),
            P(("dp", "expert")),
            P(),
            P("expert", None, None),
            P("expert", None, None),
        ),
        out_specs=(
            P(("dp", "expert"), None),
            P("expert", "dp", None),
            P("expert", "dp", None),
            P(None, "expert"),
        ),
        check_vma=False,
    )
```

```python
import functools

import jax
import jax.numpy as jnp
from jax import lax
from jax.experimental import pallas as pl
from jax.experimental.pallas import tpu as pltpu
from jax.sharding import PartitionSpec as P

MESH = pl.DeviceIdType.MESH
TRAIL = (((1,), (1,)), ((), ()))
ROWS = (((0,), (0,)), ((), ()))
WAVES = (
    ((0, 0), (2, 2), (2, 0), (0, 2)),
    ((2, 1), (2, 3), (0, 1), (0, 3)),
    ((1, 2), (3, 2), (1, 0), (3, 0)),
    ((1, 1), (3, 3), (1, 3), (3, 1)),
)
STEPS = tuple(
    (dz, dx, dc) if dc == 0 else (-dz % 4, -dx % 4, dc)
    for wave in WAVES
    for dz, dx in wave
    for dc in (0, 1)
)
COUNTS = tuple(2 * len(wave) for wave in WAVES)
FIRST = tuple(sum(COUNTS[:w]) for w in range(len(WAVES)))
SELF = STEPS.index((0, 0, 0))
N_WAVES = len(WAVES)
BLOCK = 16
AHEAD = 2
CHUNKS = tuple(
    tuple(range(first, first + count, count if w < N_WAVES - 1 else count // 2))
    for w, (first, count) in enumerate(zip(FIRST, COUNTS))
)
CHUNK_OF = tuple(
    sum(1 for chunks in CHUNKS for start in chunks if start <= k) - 1 for k in range(len(STEPS))
)
WAVE_OF = tuple(sum(1 for first in FIRST if first <= k) - 1 for k in range(len(STEPS)))
N_CHUNKS = CHUNK_OF[-1] + 1
PIECES = 8


def shifted(me, step, sign):
    dz, dx, dc = step
    z, x, c = me // 8, (me // 2) % 4, me % 2
    other = (c + dc) % 2
    swap = c if sign > 0 else other
    z = (z + sign * (dz + swap * (dx - dz)) + 4) % 4
    x = (x + sign * (dx + swap * (dz - dx)) + 4) % 4
    return (z * 4 + x) * 2 + other


def gelu_pair(values):
    inner = 0.7978845608 * (values + 0.044715 * values * values * values)
    tangent = jnp.tanh(inner)
    result = 0.5 * values * (1.0 + tangent)
    slope = 0.5 * (1.0 + tangent) + 0.5 * values * (1.0 - tangent * tangent) * 0.7978845608 * (
        1.0 + 3.0 * 0.044715 * values * values
    )
    return (result, slope)


def kernel(
    tokens, grads, slots, counts, router, up_hbm, down_hbm,
    tokens_grad, up_out, down_out, terms_out,
    pick, pick_back, scaled, column,
    x_send, g_send, x_in, g_in, r_in, w_up, w_down, act, slope, dpre, logit,
    x_far, dpre_far, g_far, act_far, up_send, down_send, up_got, down_got, own_sum,
    terms_a, terms_b,
    w_sem, xs_sem, xr_sem, gs_sem, gr_sem, rs_sem, rr_sem,
    xfs_sem, xfr_sem, dfs_sem, dfr_sem, gfs_sem, gfr_sem, afs_sem, afr_sem,
    ups_sem, upr_sem, dns_sem, dnr_sem, ts_sem, tr_sem, out_sem,
):
    shard = lax.axis_index("dp")
    me = lax.axis_index("expert")
    mate_a = shard + 1 - 2 * (shard % 2)
    mate_b = 3 - shard
    far = 3 - mate_a
    width = tokens.shape[1]
    hidden = act.shape[1]
    piece = width // 4
    step_rows = piece // PIECES

    load_up = pltpu.make_async_copy(up_hbm, w_up, w_sem.at[0])
    load_down = pltpu.make_async_copy(down_hbm, w_down, w_sem.at[1])
    load_up.start()
    load_down.start()

    barrier = pltpu.get_barrier_semaphore()
    for step in STEPS:
        if step != (0, 0, 0):
            pl.semaphore_signal(
                barrier, inc=1, device_id=(shard, shifted(me, step, 1)), device_id_type=MESH
            )
    pl.semaphore_signal(barrier, inc=1, device_id=(mate_a, me), device_id_type=MESH)
    pl.semaphore_signal(barrier, inc=1, device_id=(mate_b, me), device_id_type=MESH)

    def span(w):
        return pl.ds(FIRST[w] * BLOCK, COUNTS[w] * BLOCK)

    def columns(index, size=piece, offset=0):
        return pl.ds(pl.multiple_of(index * piece + offset, 128), size)

    def arrived(ref, sem):
        pltpu.make_async_copy(ref, ref, sem).wait()

    def remote(src, dst, send, recv, device):
        copy = pltpu.make_async_remote_copy(
            src_ref=src, dst_ref=dst, send_sem=send, recv_sem=recv,
            device_id=device, device_id_type=MESH,
        )
        copy.start()

    def travels(w):
        if FIRST[w] == SELF:
            return pl.ds((SELF + 1) * BLOCK, (COUNTS[w] - 1) * BLOCK)
        return span(w)

    def chunk_rows(start, traveled):
        count = sum(1 for k in CHUNK_OF if k == CHUNK_OF[start])
        skip = 1 if traveled and start == SELF else 0
        return pl.ds((start + skip) * BLOCK, (count - skip) * BLOCK)

    def send_blocks(w, src, dst, send, recv, tags):
        for k in range(FIRST[w], FIRST[w] + COUNTS[w]):
            rows = pl.ds(k * BLOCK, BLOCK)
            if k == SELF:
                dst[rows, :] = src[rows, :]
            else:
                remote(
                    src.at[rows], dst.at[rows], send.at[w], recv.at[tags[k]],
                    (shard, shifted(me, STEPS[k], 1)),
                )

    def return_blocks(w, src, dst, send, recv):
        for k in range(FIRST[w], FIRST[w] + COUNTS[w]):
            rows = pl.ds(k * BLOCK, BLOCK)
            home = pl.ds(pl.multiple_of(me * BLOCK, BLOCK), BLOCK)
            if k == SELF:
                dst[home, :] = src[rows, :]
            else:
                remote(
                    src.at[rows], dst.at[home], send.at[w], recv.at[w],
                    (shard, shifted(me, STEPS[k], -1)),
                )

    def add_terms(w):
        rows = span(w)
        for n in range(8):
            cols = pl.ds(n * 512, 512)
            value = jnp.sum(
                x_in[rows, cols].astype(jnp.float32) * logit[rows, :], axis=0, keepdims=True
            )
            terms_a[0:1, cols] = value if w == 0 else terms_a[0:1, cols] + value

    def give_back(w):
        rows = span(w)
        arrived(x_send.at[travels(w)], xs_sem.at[w])

        @pl.loop(0, 8)
        def _(n):
            cols = pl.ds(pl.multiple_of(n * 512, 512), 512)
            partial = lax.dot_general(
                dpre[rows, :], w_up[cols, :], TRAIL, preferred_element_type=jnp.float32
            )
            partial = partial + logit[rows, :] * column[:, cols]
            x_send[rows, cols] = partial.astype(jnp.bfloat16)

    def wave_steps(w):
        return [shifted(me, STEPS[k], 1) for k in range(FIRST[w], FIRST[w] + COUNTS[w])]

    def wave_picks(w):
        return [pick[pl.ds(pl.multiple_of(to * BLOCK, BLOCK), BLOCK), :] for to in wave_steps(w)]

    def select_tokens(w):
        chosen = jnp.concatenate(wave_picks(w), axis=0)

        @pl.loop(0, 4)
        def _(n):
            cols = columns(n)
            picked = jnp.dot(chosen, tokens[:, cols], preferred_element_type=jnp.float32)
            x_send[span(w), cols] = picked.astype(jnp.bfloat16)

    def select_grads(w):
        picks = wave_picks(w)
        chosen = jnp.concatenate(picks, axis=0)
        weight = jnp.concatenate(
            [
                jnp.sum(one.astype(jnp.float32) * scaled[pl.ds(to, 1), :], axis=1, keepdims=True)
                for one, to in zip(picks, wave_steps(w))
            ],
            axis=0,
        )

        @pl.loop(0, 4)
        def _(n):
            cols = columns(n)
            picked = jnp.dot(chosen, grads[:, cols], preferred_element_type=jnp.float32)
            g_send[span(w), cols] = (weight * picked).astype(jnp.bfloat16)

    tok_rows = tokens.shape[0]
    places = lax.broadcasted_iota(jnp.int32, (tok_rows, slots.shape[1]), 0)
    hits = jnp.where(places == slots[...], 1.0, 0.0)
    pick_back[...] = hits.astype(jnp.bfloat16)
    pick[...] = hits.T.astype(jnp.bfloat16)
    select_tokens(0)
    pl.semaphore_wait(barrier, len(STEPS) + 1)
    send_blocks(0, x_send, x_in, xs_sem, xr_sem, WAVE_OF)

    logits = jnp.zeros((router.shape[0], tok_rows), jnp.float32)
    rest = router[...]
    for _ in range(3):
        head = rest.astype(jnp.bfloat16)
        rest = rest - head.astype(jnp.float32)
        logits = logits + lax.dot_general(
            head, tokens[...], TRAIL, preferred_element_type=jnp.float32
        )
    tallies = jnp.maximum(counts[...], 1).astype(jnp.float32)
    scaled[...] = jax.nn.sigmoid(logits) / tallies
    column[...] = router[pl.ds(me, 1), :]
    def send_tokens(w):
        select_tokens(w)
        send_blocks(w, x_send, x_in, xs_sem, xr_sem, WAVE_OF)

    def send_grads(w):
        select_grads(w)
        send_blocks(w, g_send, g_in, gs_sem, gr_sem, CHUNK_OF)

    send_grads(0)
    for w in range(1, AHEAD):
        send_tokens(w)
        send_grads(w)

    load_up.wait()
    load_down.wait()
    for w in range(N_WAVES):
        rows = span(w)
        wave_rows = COUNTS[w] * BLOCK
        arrived(x_in.at[travels(w)], xr_sem.at[w])
        if w + AHEAD < N_WAVES:
            send_tokens(w + AHEAD)
        for slot, index in ((1, far), (0, mate_a)):
            remote(
                x_in.at[rows, columns(index)], x_far.at[slot, rows],
                xfs_sem.at[w], xfr_sem.at[w], (mate_a, me),
            )

        @pl.loop(0, 4)
        def _(n):
            cols = pl.ds(pl.multiple_of(n * 256, 256), 256)
            pre = jnp.dot(x_in[rows, :], w_up[:, cols], preferred_element_type=jnp.float32)
            active, bend = gelu_pair(pre)
            act[rows, cols] = active.astype(jnp.bfloat16)
            slope[0:wave_rows, cols] = bend

        remote(act.at[rows], act_far.at[rows], afs_sem.at[w], afr_sem.at[w], (mate_b, me))
        gate = jnp.zeros((wave_rows, 1), jnp.float32)
        for n in range(4):
            cols = pl.ds(n * piece, piece)
            gate = gate + jnp.sum(
                x_in[rows, cols].astype(jnp.float32) * column[:, cols], axis=1, keepdims=True
            )
        closed = 1.0 - jax.nn.sigmoid(gate)
        for start in CHUNKS[w]:
            tag = CHUNK_OF[start]
            arrived(g_in.at[chunk_rows(start, True)], gr_sem.at[tag])
            some = chunk_rows(start, False)
            for slot, index in ((1, far), (0, mate_b)):
                remote(
                    g_in.at[some, columns(index)], g_far.at[slot, some],
                    gfs_sem.at[tag], gfr_sem.at[tag], (mate_b, me),
                )
        if w + AHEAD < N_WAVES:
            send_grads(w + AHEAD)
            if w + AHEAD == N_WAVES - 1:
                for early in range(w):
                    return_blocks(early, x_send, r_in, rs_sem, rr_sem)
        logit[rows, :] = jnp.zeros((wave_rows, 1), jnp.float32)

        @pl.loop(0, 4)
        def _(n):
            cols = pl.ds(pl.multiple_of(n * 256, 256), 256)
            back = jnp.dot(g_in[rows, :], w_down[:, cols], preferred_element_type=jnp.float32)
            logit[rows, :] += jnp.sum(
                act[rows, cols].astype(jnp.float32) * back, axis=1, keepdims=True
            )
            dpre[rows, cols] = (back * slope[0:wave_rows, cols]).astype(jnp.bfloat16)

        remote(dpre.at[rows], dpre_far.at[rows], dfs_sem.at[w], dfr_sem.at[w], (mate_a, me))
        logit[rows, :] = logit[rows, :] * closed
        give_back(w)
        if w + AHEAD >= N_WAVES - 1:
            return_blocks(w, x_send, r_in, rs_sem, rr_sem)
        if w < N_WAVES - 1:
            add_terms(w)

    def product(left, index, right, left_far, slot, right_far, i, n):
        cols = pl.ds(pl.multiple_of(n * 512, 512), 512)
        offset = i * step_rows
        near = lax.dot_general(
            left[:, columns(index, step_rows, offset)], right[:, cols], ROWS,
            preferred_element_type=jnp.float32,
        )
        other = lax.dot_general(
            left_far[slot, :, pl.ds(offset, step_rows)], right_far[:, cols], ROWS,
            preferred_element_type=jnp.float32,
        )
        return cols, near + other

    def up_piece(i):
        part = pl.ds(i * step_rows, step_rows)

        @pl.loop(0, 2)
        def _(n):
            cols, value = product(x_in, mate_b, dpre, x_far, 1, dpre_far, i, n)
            up_send[part, cols] = value.astype(jnp.bfloat16)

        remote(up_send.at[part], up_got.at[part], ups_sem.at[i], upr_sem.at[i], (mate_b, me))

    def down_piece(i):
        part = pl.ds(i * step_rows, step_rows)

        @pl.loop(0, 2)
        def _(n):
            cols, value = product(g_in, mate_a, act, g_far, 1, act_far, i, n)
            down_send[part, cols] = value.astype(jnp.bfloat16)

        remote(down_send.at[part], down_got.at[part], dns_sem.at[i], dnr_sem.at[i], (mate_a, me))

    for chunks in CHUNKS:
        for start in chunks:
            arrived(g_far.at[:, chunk_rows(start, False)], gfr_sem.at[CHUNK_OF[start]])
    for w in range(N_WAVES):
        arrived(act_far.at[span(w)], afr_sem.at[w])
    down_piece(0)
    add_terms(N_WAVES - 1)
    remote(terms_a.at[0:1], terms_a.at[1:2], ts_sem.at[0], tr_sem.at[0], (mate_a, me))
    for w in range(N_WAVES):
        arrived(x_far.at[:, span(w)], xfr_sem.at[w])
        arrived(dpre_far.at[span(w)], dfr_sem.at[w])
    up_piece(0)
    for i in range(1, PIECES):
        down_piece(i)
        up_piece(i)
        if i == 1:
            arrived(terms_a.at[1:2], tr_sem.at[0])
            terms_b[0:1, :] = terms_a[0:1, :] + terms_a[1:2, :]
            remote(terms_b.at[0:1], terms_b.at[1:2], ts_sem.at[1], tr_sem.at[1], (mate_b, me))

    for i in range(PIECES):
        part = pl.ds(i * step_rows, step_rows)

        @pl.loop(0, 2)
        def _(n):
            cols, value = product(g_in, shard, act, g_far, 0, act_far, i, n)
            own_sum[0, :, cols] = value
            cols, value = product(x_in, shard, dpre, x_far, 0, dpre_far, i, n)
            own_sum[1, :, cols] = value

        if i == PIECES - 1:
            arrived(terms_b.at[1:2], tr_sem.at[1])
            terms_out[...] = terms_b[0:1, :] + terms_b[1:2, :]
            for w in range(N_WAVES):
                arrived(r_in.at[travels(w)], rr_sem.at[w])

            @pl.loop(0, 8)
            def _(n):
                cols = pl.ds(pl.multiple_of(n * 512, 512), 512)
                tokens_grad[:, cols] = jnp.dot(
                    pick_back[...], r_in[:, cols], preferred_element_type=jnp.float32
                ).astype(jnp.bfloat16)

        arrived(down_got.at[part], dnr_sem.at[i])
        down_got[part, :] = (own_sum[0] + down_got[part, :].astype(jnp.float32)).astype(
            jnp.bfloat16
        )
        pltpu.make_async_copy(down_got.at[part], down_out.at[part], out_sem.at[0, i]).start()
        arrived(up_got.at[part], upr_sem.at[i])
        up_got[part, :] = (own_sum[1] + up_got[part, :].astype(jnp.float32)).astype(jnp.bfloat16)
        pltpu.make_async_copy(up_got.at[part], up_out.at[part], out_sem.at[1, i]).start()

    for w in range(N_WAVES):
        arrived(g_send.at[travels(w)], gs_sem.at[w])
        arrived(x_send.at[travels(w)], rs_sem.at[w])
        arrived(x_far.at[:, span(w)], xfs_sem.at[w])
        arrived(act.at[span(w)], afs_sem.at[w])
        arrived(dpre.at[span(w)], dfs_sem.at[w])
    for chunks in CHUNKS:
        for start in chunks:
            arrived(g_far.at[:, chunk_rows(start, False)], gfs_sem.at[CHUNK_OF[start]])
    arrived(terms_a.at[0:1], ts_sem.at[0])
    arrived(terms_b.at[0:1], ts_sem.at[1])
    for i in range(PIECES):
        part = pl.ds(i * step_rows, step_rows)
        arrived(down_send.at[part], dns_sem.at[i])
        arrived(up_send.at[part], ups_sem.at[i])
        pltpu.make_async_copy(down_got.at[part], down_out.at[part], out_sem.at[0, i]).wait()
        pltpu.make_async_copy(up_got.at[part], up_out.at[part], out_sem.at[1, i]).wait()


def hand_over(first, second, third, first_out, second_out, third_out, a, b, c, in_sem, sem):
    moves = []
    for n, (src, mid, dst) in enumerate(
        ((first, a, first_out), (second, b, second_out), (third, c, third_out))
    ):
        rows = src.shape[0] // 4
        for i in range(4):
            part = pl.ds(i * rows, rows)
            load = pltpu.make_async_copy(src.at[part], mid.at[part], in_sem.at[n, i])
            load.start()
            moves.append((load, mid.at[part], dst.at[part], sem.at[n, i]))
    stores = []
    for load, mid, dst, one in moves:
        load.wait()
        store = pltpu.make_async_copy(mid, dst, one)
        store.start()
        stores.append(store)
    for store in stores:
        store.wait()


def on_device(tokens, out_grad, route_slots, expert_counts, router_weight, up_weight, down_weight):
    tok_rows, width = tokens.shape
    hidden = up_weight.shape[2]
    piece = width // 4
    slots = route_slots[0, 0]
    experts, per_slot = slots.shape
    received = experts * per_slot
    slots = slots.reshape(1, received)
    counts = expert_counts.reshape(1, tok_rows)
    router = router_weight.T

    half = jnp.bfloat16
    vmem = pl.BlockSpec(memory_space=pltpu.VMEM)
    anywhere = pl.BlockSpec(memory_space=pl.ANY)
    dma = pltpu.SemaphoreType.DMA
    rows_buffer = pltpu.VMEM((received, width), half)
    inner = pltpu.VMEM((received, hidden), half)
    halves = pltpu.VMEM((2, received, piece), half)
    square = pltpu.VMEM((piece, hidden), half)
    full = pltpu.VMEM((width, hidden), half)
    tokens_grad, up_sum, down_sum, terms = pl.pallas_call(
        kernel,
        out_shape=(
            jax.ShapeDtypeStruct((tok_rows, width), half),
            jax.ShapeDtypeStruct((piece, hidden), half),
            jax.ShapeDtypeStruct((piece, hidden), half),
            jax.ShapeDtypeStruct((1, width), jnp.float32),
        ),
        in_specs=[vmem] * 5 + [anywhere] * 2,
        out_specs=(vmem, anywhere, anywhere, vmem),
        scratch_shapes=[
            pltpu.VMEM((received, tok_rows), half), pltpu.VMEM((tok_rows, received), half),
            pltpu.VMEM((experts, tok_rows), jnp.float32), pltpu.VMEM((1, width), jnp.float32),
            rows_buffer, rows_buffer, rows_buffer, rows_buffer, rows_buffer, full, full,
            inner, pltpu.VMEM((max(COUNTS) * BLOCK, hidden), jnp.float32), inner,
            pltpu.VMEM((received, 1), jnp.float32),
            halves, inner, halves, inner, square, square, square, square,
            pltpu.VMEM((2, piece // PIECES, hidden), jnp.float32),
            pltpu.VMEM((2, width), jnp.float32), pltpu.VMEM((2, width), jnp.float32),
            dma((2,)),
        ]
        + [dma((N_WAVES,))] * 3 + [dma((N_CHUNKS,))] + [dma((N_WAVES,))] * 2
        + [dma((N_WAVES,))] * 4 + [dma((N_CHUNKS,))] * 2 + [dma((N_WAVES,))] * 2
        + [dma((PIECES,))] * 4
        + [dma((2,)), dma((2,)), dma((2, PIECES))],
        compiler_params=pltpu.CompilerParams(
            collective_id=0, has_side_effects=True, vmem_limit_bytes=67043328
        ),
        name="exchange",
    )(tokens, out_grad, slots, counts, router, up_weight[0], down_weight[0])
    results = (tokens_grad, up_sum, down_sum)
    tokens_grad, up_sum, down_sum = pl.pallas_call(
        hand_over,
        out_shape=tuple(jax.ShapeDtypeStruct(one.shape, one.dtype) for one in results),
        in_specs=[anywhere] * 3,
        out_specs=(anywhere,) * 3,
        scratch_shapes=[pltpu.VMEM(one.shape, one.dtype) for one in results]
        + [dma((3, 4)), dma((3, 4))],
        name="hand_over",
    )(*results)
    return (tokens_grad, up_sum[None], down_sum[None], terms.reshape(width, 1))


def solution(mesh):
    return jax.shard_map(
        on_device,
        mesh=mesh,
        in_specs=(
            P(("dp", "expert"), None),
            P(("dp", "expert"), None),
            P("dp", "expert", None, None),
            P(("dp", "expert")),
            P(),
            P("expert", None, None),
            P("expert", None, None),
        ),
        out_specs=(
            P(("dp", "expert"), None),
            P("expert", "dp", None),
            P("expert", "dp", None),
            P(None, "expert"),
        ),
        check_vma=False,
    )
```
